128 devices in a mesh: seq: 16 (over y, x_lo, core), head: 8 (over x_hi, z).
Axes of the slice: x: 4 (x_hi: 2, x_lo: 2; x = x_hi * 2 + x_lo), y: 4, z: 4, core: 2. Of those that a mesh axis runs over, the one named last changes fastest.
Arguments:
- queries: bfloat16 [8192, 8192], P('seq', 'head'), may hold values from -60 to 60
- keys: bfloat16 [8192, 1024], P('seq', 'head'), may hold values from -6 to 6
- values: bfloat16 [8192, 1024], P('seq', 'head'), may hold values from -6 to 6
- positions: int32 [8192], P('seq'), may hold values from 0 to 8191, as said below
- out_weight: bfloat16 [8192, 8192], P('head', 'seq'), may hold values from -0.25 to 0.25
Outputs:
- mixed: bfloat16 [8192, 8192], P('seq', 'head')
The draws below stay inside these ranges and needn't reach their ends.
Inputs may be any that keep to these rules, and one draw needn't show every extreme that they name: positions is a permutation of the document's positions; each aligned group of 128 rows holds 128 consecutive positions in increasing order.
All inputs are finite; a program needn't handle non-finite values.
Results may differ from the reference program's by a relative error of at most 0.018.
Values may be sent and summed in bfloat16 or wider, within the bound.
No kernel may reach another device: no remote copies, remote signals or barrier semaphores. Data moves between devices by JAX's collectives and lax.ppermute only.
A program may use at most 128 MiB of HBM per device.

```python
import math
import jax
import jax.numpy as jnp
from jax import lax

D = 8192
HEADS = 64
KV_HEADS = 8
HD = 128
L_DEV = 512
BLK = 128
SEQ = 8192
N_SEQ = 16
N_HEAD = 8


def shared_pair(key):
    key_base = jax.random.fold_in(key, 11)
    key_query = jax.random.fold_in(key, 12)
    key_strength = jax.random.fold_in(key, 14)
    base = jax.random.truncated_normal(key_base, -6.0, 6.0, (SEQ, KV_HEADS * HD), jnp.float32)
    query_raw = 2.0 * jax.random.truncated_normal(key_query, -6.0, 6.0, (SEQ, HEADS * HD), jnp.float32)
    selected = jnp.zeros((SEQ,), bool)
    strength = 10.0 * jax.random.randint(key_strength, (SEQ,), 1, 4).astype(jnp.float32)
    ratio = HEADS // KV_HEADS
    spread = jnp.repeat(base.reshape(SEQ, KV_HEADS, 1, HD), ratio, axis=2).reshape(SEQ, HEADS * HD)
    queries = jnp.where(selected[:, None], strength[:, None] * spread, query_raw)
    following = jnp.roll(selected, -1)
    following_strength = jnp.roll(strength, -1)
    keys = jnp.where(following[:, None], jnp.roll(base, -1, 0) * (1.0 - 0.2 / following_strength[:, None]), base)
    return (queries, keys)


def draw_queries(key, part):
    return shared_pair(key)[0].astype(jnp.bfloat16)


def draw_keys(key, part):
    return shared_pair(key)[1].astype(jnp.bfloat16)


def draw_positions(key, part):
    blocks = jax.random.permutation(jax.random.fold_in(key, 21), SEQ // BLK).astype(jnp.int32)
    row_index = jnp.arange(SEQ, dtype=jnp.int32)
    return blocks[row_index // BLK] * BLK + row_index % BLK


def level_of(key, extent, shards, smallest, high):
    def one(axis_at, shards_of):
        steps = jax.random.uniform(jax.random.fold_in(jax.random.fold_in(key, 6), axis_at), (shards_of,), jnp.float32, smallest / len(shards), high / len(shards))
        return jnp.repeat(jnp.exp(steps), extent[axis_at] // shards_of).reshape((-1,) + (1,) * (len(extent) - axis_at - 1))

    loudness = one(*shards[0])
    for cut in shards[1:]:
        loudness = loudness * one(*cut)
    return loudness


def scatter_about(stream_key, shape, deviation, bound, cuts=(), held_as=jnp.bfloat16):
    entries = jax.random.normal(stream_key, shape, jnp.float32) * deviation
    if len(cuts) > 0:
        entries = level_of(stream_key, shape, cuts, -0.22, 0.18) * entries
    return jnp.clip(entries, min=-bound, max=bound).astype(held_as)


def setup_inputs(seed: int = 0) -> dict:
    streams_of = jax.random.split(jax.random.key(seed), 6)
    return {
        "queries": draw_queries(jax.random.fold_in(streams_of[5], 71), 0),
        "keys": draw_keys(jax.random.fold_in(streams_of[5], 71), 0),
        "values": scatter_about(streams_of[2], (SEQ, KV_HEADS * HD), 1.0, 6.0, ((0, 16), (1, 8))),
        "positions": draw_positions(jax.random.fold_in(streams_of[5], 71), 0),
        "out_weight": scatter_about(streams_of[4], (HEADS * HD, D), (HEADS * HD // 16) ** -0.5, 0.25, ((0, 8), (1, 16))),
    }


masked_score = -1e+30

def reference(queries, keys, values, positions, out_weight):
    ratio = HEADS // KV_HEADS
    scale = 1.0 / math.sqrt(HD)

    def head_out(head):
        group = head // ratio
        query_head = lax.dynamic_slice_in_dim(queries, (head * HD).astype(jnp.int32), HD, 1)
        key_head = lax.dynamic_slice_in_dim(keys, (group * HD).astype(jnp.int32), HD, 1)
        value_head = lax.dynamic_slice_in_dim(values, (group * HD).astype(jnp.int32), HD, 1)

        def rows_out(index):
            start = (index * L_DEV).astype(jnp.int32)
            query_rows = lax.dynamic_slice_in_dim(query_head, start, L_DEV, 0)
            query_pos = lax.dynamic_slice_in_dim(positions, start, L_DEV, 0)
            scores = jnp.dot(query_rows, key_head.T, preferred_element_type=jnp.float32) * scale
            visible = positions[None, :] <= query_pos[:, None]
            scores = jnp.where(visible, scores, masked_score)
            top = lax.optimization_barrier(jnp.max(scores, axis=-1, keepdims=True))
            weights = jnp.where(visible, jnp.exp(scores - top), 0.0)
            denominator = lax.optimization_barrier(jnp.sum(weights, axis=-1, keepdims=True))
            summed = jnp.dot(weights.astype(jnp.bfloat16), value_head, preferred_element_type=jnp.float32)
            return (summed / denominator).astype(jnp.bfloat16)
        return lax.map(rows_out, jnp.arange(N_SEQ, dtype=jnp.int32))
    outputs = lax.map(head_out, jnp.arange(HEADS, dtype=jnp.int32))
    attention = jnp.transpose(outputs, (1, 2, 0, 3)).reshape(SEQ, HEADS * HD)
    width = HEADS * HD // N_HEAD
    total = jnp.zeros((SEQ, D), jnp.float32)
    for group in range(N_HEAD):
        partial_term = jnp.dot(attention[:, group * width:(group + 1) * width], out_weight[group * width:(group + 1) * width], preferred_element_type=jnp.float32)
        partial_term = lax.optimization_barrier(partial_term.astype(jnp.bfloat16))
        total = total + partial_term.astype(jnp.float32)
    return total.astype(jnp.bfloat16)
```

```python
import functools
import math

import jax
import jax.numpy as jnp
from jax import lax
from jax.experimental import pallas as pl
from jax.experimental.pallas import tpu as pltpu
from jax.sharding import Mesh
from jax.sharding import PartitionSpec as P

HD = 128
BLK = 128
TILE = 512
AXES = ("y", "xl", "c", "xh", "z")
SIZES = {"y": 4, "xl": 2, "c": 2, "xh": 2, "z": 4}
masked_score = -1e30
VMEM_BYTES = 56 << 20


def move(block, axes, target):
    sizes = [SIZES[a] for a in axes]
    count = math.prod(sizes)
    route = []
    for i in range(count):
        rest, at = i, []
        for size in reversed(sizes):
            at.append(rest % size)
            rest //= size
        to = target(*reversed(at))
        j = 0
        for t, size in zip(to, sizes):
            j = j * size + t % size
        route.append((i, j))
    return lax.ppermute(block, axes, route)


def sort_blocks(slot_ref, *refs):
    sources, (keys_ref, values_ref, sem) = refs[:16], refs[16:]
    copies = []
    for r in range(16):
        for b in range(4):
            slot = pl.multiple_of(slot_ref[r * 4 + b] * BLK, BLK)
            for part, sorted_ref in enumerate((keys_ref, values_ref)):
                copies.append(
                    pltpu.make_async_copy(
                        sources[r].at[pl.ds(part * 512 + b * BLK, BLK), :],
                        sorted_ref.at[pl.ds(slot, BLK), :],
                        sem.at[part, r * 4 + b],
                    )
                )
    for copy in copies:
        copy.start()
    for copy in copies:
        copy.wait()


def sorted_kv(slots, sources):
    anywhere = pl.BlockSpec(memory_space=pl.ANY)
    inside = pl.BlockSpec(memory_space=pltpu.VMEM)
    sorted_shape = jax.ShapeDtypeStruct((64 * BLK, HD), jnp.bfloat16)
    return pl.pallas_call(
        sort_blocks,
        out_shape=(sorted_shape, sorted_shape),
        in_specs=[pl.BlockSpec(memory_space=pltpu.SMEM)] + [anywhere] * 16,
        out_specs=(inside, inside),
        scratch_shapes=[pltpu.SemaphoreType.DMA((2, 64))],
        cost_estimate=pl.CostEstimate(flops=0, bytes_accessed=8 << 20, transcendentals=0),
        name="sort_blocks",
    )(slots, *sources)


def attend(chunk, own_ref, q_ref, keys_ref, values_ref, out_ref, k_s, v_s, q_s, s_s, acc, best, total, sem):
    rows = 8 * BLK
    factor = math.log2(math.e) / math.sqrt(HD)
    block = own_ref[chunk]
    tiles = block // (TILE // BLK) + 1

    def copies(j):
        at = pl.multiple_of(j * TILE, TILE)
        return (
            pltpu.make_async_copy(
                keys_ref.at[pl.ds(at, TILE), :], k_s.at[pl.ds(at, TILE), :], sem.at[0, j]
            ),
            pltpu.make_async_copy(
                values_ref.at[pl.ds(at, TILE), :], v_s.at[pl.ds(at, TILE), :], sem.at[1, j]
            ),
        )

    def begin(j, carry):
        for copy in copies(j):
            copy.start()
        return carry

    lax.fori_loop(0, tiles, begin, 0)
    for h in range(8):
        q_s[h * BLK : (h + 1) * BLK, :] = q_ref[:, h * HD : (h + 1) * HD]
    acc[...] = jnp.zeros_like(acc)
    best[...] = jnp.full_like(best, masked_score)
    total[...] = jnp.zeros_like(total)

    def score(j):
        at = pl.multiple_of(j * TILE, TILE)
        return lax.dot_general(
            k_s[pl.ds(at, TILE), :],
            q_s[...],
            (((1,), (1,)), ((), ())),
            preferred_element_type=jnp.float32,
        )

    def absorb(j, scores):
        at = pl.multiple_of(j * TILE, TILE)
        old = best[...]
        new = jnp.maximum(old, jnp.max(scores, axis=0, keepdims=True))
        weights = jnp.exp2((scores - new) * factor)
        shrink = jnp.exp2((old - new) * factor)
        total[...] = total[...] * shrink + jnp.sum(weights, axis=0, keepdims=True)
        best[...] = new
        acc[...] = acc[...] * shrink + lax.dot_general(
            v_s[pl.ds(at, TILE), :],
            weights.astype(jnp.bfloat16),
            (((0,), (0,)), ((), ())),
            preferred_element_type=jnp.float32,
        )

    copies(0)[0].wait()
    s_s[0] = score(0)

    def full_tile(j, carry):
        copies(j + 1)[0].wait()
        copies(j)[1].wait()
        scores = s_s[j % 2]
        s_s[(j + 1) % 2] = score(j + 1)
        absorb(j, scores)
        return carry

    lax.fori_loop(0, tiles - 1, full_tile, 0)
    last = tiles - 1
    copies(last)[1].wait()
    key_at = last * TILE + lax.broadcasted_iota(jnp.int32, (TILE, rows), 0)
    query_at = block * BLK + lax.broadcasted_iota(jnp.int32, (TILE, rows), 1) % BLK
    absorb(last, jnp.where(key_at <= query_at, s_s[last % 2], masked_score))
    result = acc[...] / total[...]
    for h in range(8):
        part = result[:, h * BLK : (h + 1) * BLK]
        out_ref[:, h * HD : (h + 1) * HD] = part.T.astype(jnp.bfloat16)


def attention(chunk, own, queries, keys, values):
    anywhere = pl.BlockSpec(memory_space=pl.ANY)
    total = 64 * BLK
    rows = 8 * BLK
    return pl.pallas_call(
        functools.partial(attend, chunk),
        out_shape=jax.ShapeDtypeStruct((BLK, rows), jnp.bfloat16),
        grid=(1,),
        in_specs=[
            pl.BlockSpec(memory_space=pltpu.SMEM),
            pl.BlockSpec((BLK, rows), lambda i: (chunk, 0)),
            anywhere,
            anywhere,
        ],
        out_specs=pl.BlockSpec((BLK, rows), lambda i: (0, 0)),
        scratch_shapes=[
            pltpu.VMEM((total, HD), jnp.bfloat16),
            pltpu.VMEM((total, HD), jnp.bfloat16),
            pltpu.VMEM((rows, HD), jnp.bfloat16),
            pltpu.VMEM((2, TILE, rows), jnp.float32),
            pltpu.VMEM((HD, rows), jnp.float32),
            pltpu.VMEM((1, rows), jnp.float32),
            pltpu.VMEM((1, rows), jnp.float32),
            pltpu.SemaphoreType.DMA((2, total // TILE)),
        ],
        compiler_params=pltpu.CompilerParams(vmem_limit_bytes=VMEM_BYTES),
        cost_estimate=pl.CostEstimate(
            flops=10_000_000_000, bytes_accessed=1 << 22, transcendentals=0
        ),
        name="attend",
    )(own, queries, keys, values)


def project_body(n_chunks, has_sum, *refs):
    pieces, rest = refs[: 4 * n_chunks], refs[4 * n_chunks :]
    if has_sum:
        w_ref, sum_ref, out_ref, a_s, sem = rest
    else:
        w_ref, out_ref, a_s, sem = rest

    @pl.when(pl.program_id(0) == 0)
    def _():
        copies = [
            pltpu.make_async_copy(
                pieces[i * 4 + dz],
                a_s.at[pl.ds(i * BLK, BLK), pl.ds(dz * 1024, 1024)],
                sem.at[i * 4 + dz],
            )
            for i in range(n_chunks)
            for dz in range(4)
        ]
        for copy in copies:
            copy.start()
        for copy in copies:
            copy.wait()

    result = jnp.dot(
        a_s[...], w_ref[...].reshape(4096, 256), preferred_element_type=jnp.float32
    )
    if has_sum:
        result = result + sum_ref[...].astype(jnp.float32)
    out_ref[...] = result.astype(jnp.bfloat16)


def project(pieces, weight, other=None):
    n_chunks = len(pieces)
    rows = n_chunks * BLK
    anywhere = pl.BlockSpec(memory_space=pl.ANY)
    tile = pl.BlockSpec((rows, 256), lambda n: (0, n))
    flat = [piece for chunk in pieces for piece in chunk]
    return pl.pallas_call(
        functools.partial(project_body, n_chunks, other is not None),
        out_shape=jax.ShapeDtypeStruct((rows, 1024), jnp.bfloat16),
        grid=(4,),
        in_specs=[anywhere] * len(flat)
        + [pl.BlockSpec((8, None, 512, 256), lambda n: (0, n // 2, 0, n % 2))]
        + ([tile] if other is not None else []),
        out_specs=tile,
        scratch_shapes=[
            pltpu.VMEM((rows, 4096), jnp.bfloat16),
            pltpu.SemaphoreType.DMA((4 * n_chunks,)),
        ],
        compiler_params=pltpu.CompilerParams(vmem_limit_bytes=VMEM_BYTES),
        cost_estimate=pl.CostEstimate(
            flops=2 * rows * 4096 * 1024, bytes_accessed=10 << 20, transcendentals=0
        ),
        name="project",
    )(*flat, weight.reshape(8, 2, 512, 512), *([other] if other is not None else []))


def spread_target(half):
    def target(y, xl, xh, z):
        plane = (y % 2) * 2 + xl
        other = (y // 2) ^ xh
        part = half if other else 1 - half
        return ((z - plane) % 4, part, xh, plane)

    return target


def per_device(queries, keys, values, positions, out_weight):
    y, xl, xh = lax.axis_index("y"), lax.axis_index("xl"), lax.axis_index("xh")
    own = positions[::BLK] // BLK
    ids = jnp.broadcast_to(own.astype(jnp.bfloat16)[None, :, None], (4, 4, HD)).reshape(16, HD)
    packet = jnp.concatenate([keys, values, ids])
    received = [packet] + [
        move(packet, ("y", "xl"), lambda a, b, dy=dy, dx=dx: (a + dy, b + dx))
        for dy, dx in ((1, 0), (3, 0), (0, 1), (1, 1), (3, 1), (2, 0), (2, 1))
    ]
    out_weight, received[1] = lax.optimization_barrier((out_weight, received[1]))

    other = (y // 2) ^ xh
    first = lax.dynamic_slice_in_dim(out_weight, (1 - other) * 512, 512, 0)
    second = lax.dynamic_slice_in_dim(out_weight, other * 512, 512, 0)
    plane = ("y", "xl", "xh", "z")
    got_first = move(first, plane, spread_target(0))
    got_second = move(second, plane, spread_target(1))
    for_partner = jnp.where(xl == 0, got_first, got_second)
    for_self = jnp.where(xl == 0, got_second, got_first)
    ready = lax.optimization_barrier((for_partner, for_self, *received))
    for_partner, for_self, received = ready[0], ready[1], list(ready[2:])
    weight_partner = lax.all_gather(for_partner, ("y", "xl", "c"))
    weight_self = lax.all_gather(for_self, ("y", "xl", "c"))

    received = received + [move(r, ("c",), lambda a: (a + 1,)) for r in received]
    slots = jnp.concatenate([r[1024:1028, 0] for r in received]).astype(jnp.int32)
    sorted_keys, sorted_values = sorted_kv(slots, received)

    pieces = []
    for i in range(4):
        piece = attention(i, own, queries, sorted_keys, sorted_values)
        pieces.append([piece] + [move(piece, ("z",), lambda a, dz=dz: (a - dz,)) for dz in (1, 2, 3)])
    partner_sum = project(pieces, weight_partner)
    got_sum = move(partner_sum, ("xh",), lambda a: (a + 1,))
    return project(pieces, weight_self, got_sum)


def solution(mesh):
    split = Mesh(mesh.devices.reshape([SIZES[a] for a in AXES]), AXES)
    seq, head = ("y", "xl", "c"), ("xh", "z")
    placed = (P(seq, head), P(seq, head), P(seq, head), P(seq), P(head, seq))
    return jax.shard_map(
        per_device, mesh=split, in_specs=placed, out_specs=P(seq, head), check_vma=False
    )
```

```python
import functools
import math

import jax
import jax.numpy as jnp
from jax import lax
from jax.experimental import pallas as pl
from jax.experimental.pallas import tpu as pltpu
from jax.sharding import Mesh
from jax.sharding import PartitionSpec as P

HD = 128
BLK = 128
TILE = 512
AXES = ("y", "xl", "c", "xh", "z")
SIZES = {"y": 4, "xl": 2, "c": 2, "xh": 2, "z": 4}
masked_score = -1e30
VMEM_BYTES = 56 << 20


def move(block, axes, target):
    sizes = [SIZES[a] for a in axes]
    count = math.prod(sizes)
    route = []
    for i in range(count):
        rest, at = i, []
        for size in reversed(sizes):
            at.append(rest % size)
            rest //= size
        to = target(*reversed(at))
        j = 0
        for t, size in zip(to, sizes):
            j = j * size + t % size
        route.append((i, j))
    return lax.ppermute(block, axes, route)


def run_all(copies):
    for copy in copies:
        copy.start()
    for copy in copies:
        copy.wait()


def sort_blocks(slot_ref, mine_ref, other_ref, sorted_ref, sem):
    run_all(
        [
            pltpu.make_async_copy(
                (mine_ref, other_ref)[i // 32].at[i // 4 % 8, pl.ds(i % 4 * 2 * BLK, 2 * BLK), :],
                sorted_ref.at[slot_ref[i]],
                sem.at[i],
            )
            for i in range(64)
        ]
    )


def sorted_kv(slots, mine, other):
    anywhere = pl.BlockSpec(memory_space=pl.ANY)
    return pl.pallas_call(
        sort_blocks,
        out_shape=jax.ShapeDtypeStruct((64, 2 * BLK, HD), jnp.bfloat16),
        in_specs=[pl.BlockSpec(memory_space=pltpu.SMEM), anywhere, anywhere],
        out_specs=pl.BlockSpec(memory_space=pltpu.VMEM),
        scratch_shapes=[pltpu.SemaphoreType.DMA((64,))],
        compiler_params=pltpu.CompilerParams(vmem_limit_bytes=VMEM_BYTES),
        cost_estimate=pl.CostEstimate(flops=0, bytes_accessed=8 << 20, transcendentals=0),
        name="sort_blocks",
    )(slots, mine, other)


def attend(chunk, own_ref, order_ref, q_ref, kv_ref, out_ref, kv_s, q_s, s_s, acc, best, total, sem):
    rows = 8 * BLK
    per_tile = TILE // BLK
    factor = math.log2(math.e) / math.sqrt(HD)
    block = own_ref[order_ref[chunk]]
    tiles = block // per_tile + 1

    def copy_of(j):
        slots = pl.ds(j * per_tile, per_tile)
        return pltpu.make_async_copy(kv_ref.at[slots], kv_s.at[slots], sem.at[j])

    def begin(j, carry):
        copy_of(j).start()
        return carry

    lax.fori_loop(0, tiles, begin, 0)
    for h in range(8):
        q_s[h * BLK : (h + 1) * BLK, :] = q_ref[:, h * HD : (h + 1) * HD]
    acc[...] = jnp.zeros_like(acc)
    best[...] = jnp.full_like(best, masked_score)
    total[...] = jnp.zeros_like(total)

    def score(j):
        return lax.dot_general(
            kv_s[pl.ds(j * per_tile, per_tile), :BLK, :].reshape(TILE, HD),
            q_s[...],
            (((1,), (1,)), ((), ())),
            preferred_element_type=jnp.float32,
        )

    def absorb(j, scores):
        old = best[...]
        new = jnp.maximum(old, jnp.max(scores, axis=0, keepdims=True))
        weights = jnp.exp2((scores - new) * factor)
        shrink = jnp.exp2((old - new) * factor)
        total[...] = total[...] * shrink + jnp.sum(weights, axis=0, keepdims=True)
        best[...] = new
        acc[...] = acc[...] * shrink + lax.dot_general(
            kv_s[pl.ds(j * per_tile, per_tile), BLK:, :].reshape(TILE, HD),
            weights.astype(jnp.bfloat16),
            (((0,), (0,)), ((), ())),
            preferred_element_type=jnp.float32,
        )

    copy_of(0).wait()
    s_s[0] = score(0)

    def full_tile(j, carry):
        copy_of(j + 1).wait()
        scores = s_s[j % 2]
        s_s[(j + 1) % 2] = score(j + 1)
        absorb(j, scores)
        return carry

    lax.fori_loop(0, tiles - 1, full_tile, 0)
    last = tiles - 1
    key_at = last * TILE + lax.broadcasted_iota(jnp.int32, (TILE, rows), 0)
    query_at = block * BLK + lax.broadcasted_iota(jnp.int32, (TILE, rows), 1) % BLK
    absorb(last, jnp.where(key_at <= query_at, s_s[last % 2], masked_score))
    result = acc[...] / total[...]
    for h in range(8):
        part = result[:, h * BLK : (h + 1) * BLK]
        out_ref[:, h * HD : (h + 1) * HD] = part.T.astype(jnp.bfloat16)


def attention(chunk, own, order, queries, kv):
    rows = 8 * BLK
    return pl.pallas_call(
        functools.partial(attend, chunk),
        out_shape=jax.ShapeDtypeStruct((BLK, rows), jnp.bfloat16),
        grid_spec=pltpu.PrefetchScalarGridSpec(
            num_scalar_prefetch=2,
            grid=(1,),
            in_specs=[
                pl.BlockSpec((BLK, rows), lambda i, own, order: (order[chunk], 0)),
                pl.BlockSpec(memory_space=pl.ANY),
            ],
            out_specs=pl.BlockSpec((BLK, rows), lambda i, own, order: (0, 0)),
            scratch_shapes=[
                pltpu.VMEM((64, 2 * BLK, HD), jnp.bfloat16),
                pltpu.VMEM((rows, HD), jnp.bfloat16),
                pltpu.VMEM((2, TILE, rows), jnp.float32),
                pltpu.VMEM((HD, rows), jnp.float32),
                pltpu.VMEM((1, rows), jnp.float32),
                pltpu.VMEM((1, rows), jnp.float32),
                pltpu.SemaphoreType.DMA((64 * BLK // TILE,)),
            ],
        ),
        compiler_params=pltpu.CompilerParams(vmem_limit_bytes=VMEM_BYTES),
        cost_estimate=pl.CostEstimate(
            flops=10_000_000_000, bytes_accessed=1 << 22, transcendentals=0
        ),
        name="attend",
    )(own, order, queries, kv)


def project_partner(order_ref, *refs):
    pieces, (w_ref, out_ref, all_ref, a_s, sem) = refs[:-5], refs[-5:]
    n = pl.program_id(0)
    keep = pltpu.make_async_copy(a_s, all_ref, sem.at[len(pieces)])

    @pl.when(n == 0)
    def _():
        run_all(
            [
                pltpu.make_async_copy(
                    piece,
                    a_s.at[
                        pl.ds(pl.multiple_of(order_ref[i // 4] * BLK, BLK), BLK),
                        pl.ds(i % 4 * 1024, 1024),
                    ],
                    sem.at[i],
                )
                for i, piece in enumerate(pieces)
            ]
        )
        keep.start()

    w = w_ref[...].reshape(4096, 256)
    out = jnp.dot(a_s[...], w, preferred_element_type=jnp.float32)
    out_ref[...] = out.astype(jnp.bfloat16)

    @pl.when(n == pl.num_programs(0) - 1)
    def _():
        keep.wait()


def partner_terms(order, pieces, weight):
    return pl.pallas_call(
        project_partner,
        out_shape=(
            jax.ShapeDtypeStruct((512, 1024), jnp.bfloat16),
            jax.ShapeDtypeStruct((512, 4096), jnp.bfloat16),
        ),
        grid_spec=pltpu.PrefetchScalarGridSpec(
            num_scalar_prefetch=1,
            grid=(4,),
            in_specs=[pl.BlockSpec(memory_space=pl.ANY)] * len(pieces)
            + [pl.BlockSpec((8, None, 512, 256), lambda n, o: (0, n // 2, 0, n % 2))],
            out_specs=(
                pl.BlockSpec((512, 256), lambda n, o: (0, n)),
                pl.BlockSpec(memory_space=pl.ANY),
            ),
            scratch_shapes=[
                pltpu.VMEM((512, 4096), jnp.bfloat16),
                pltpu.SemaphoreType.DMA((len(pieces) + 1,)),
            ],
        ),
        compiler_params=pltpu.CompilerParams(vmem_limit_bytes=VMEM_BYTES),
        cost_estimate=pl.CostEstimate(
            flops=2 * 512 * 4096 * 1024, bytes_accessed=18 << 20, transcendentals=0
        ),
        name="project_partner",
    )(order, *pieces, weight)


def project_self(a_ref, w_ref, sum_ref, out_ref):
    w = w_ref[...].reshape(4096, 256)
    out = jnp.dot(a_ref[...], w, preferred_element_type=jnp.float32)
    out_ref[...] = (out + sum_ref[...].astype(jnp.float32)).astype(jnp.bfloat16)


def own_terms(rows, weight, other):
    tile = pl.BlockSpec((512, 256), lambda n: (0, n))
    return pl.pallas_call(
        project_self,
        out_shape=jax.ShapeDtypeStruct((512, 1024), jnp.bfloat16),
        grid=(4,),
        in_specs=[
            pl.BlockSpec((512, 4096), lambda n: (0, 0)),
            pl.BlockSpec((8, None, 512, 256), lambda n: (0, n // 2, 0, n % 2)),
            tile,
        ],
        out_specs=tile,
        compiler_params=pltpu.CompilerParams(vmem_limit_bytes=VMEM_BYTES),
        cost_estimate=pl.CostEstimate(
            flops=2 * 512 * 4096 * 1024, bytes_accessed=14 << 20, transcendentals=0
        ),
        name="project_self",
    )(rows, weight, other)


def spread_target(half):
    def target(y, xl, xh, z):
        plane = (y % 2) * 2 + xl
        other = (y // 2) ^ xh
        part = half if other else 1 - half
        return ((z - plane) % 4, part, xh, plane)

    return target


def swap_cores(block):
    return move(block, ("c",), lambda a: (a + 1,))


def per_device(queries, keys, values, positions, out_weight):
    y, xl, xh = lax.axis_index("y"), lax.axis_index("xl"), lax.axis_index("xh")
    own = positions[::BLK] // BLK
    index = jnp.arange(4, dtype=jnp.int32)
    rank = jnp.sum((own[None, :] < own[:, None]).astype(jnp.int32), axis=1)
    order = jnp.sum(jnp.where(rank[None, :] == index[:, None], index[None, :], 0), axis=1)
    ids = jnp.broadcast_to(own.astype(jnp.bfloat16)[None, :, None], (4, 4, HD)).reshape(16, HD)
    pairs = jnp.stack([keys.reshape(4, BLK, HD), values.reshape(4, BLK, HD)], 1)
    packet = jnp.concatenate([pairs.reshape(8 * BLK, HD), ids])
    copies = jnp.broadcast_to(packet[None], (8, *packet.shape))
    mine = lax.all_to_all(copies, ("y", "xl"), 0, 0, tiled=True)

    def later(first, *values):
        return lax.optimization_barrier((first, *values))[1:]

    other = (y // 2) ^ xh
    first = lax.dynamic_slice_in_dim(out_weight, (1 - other) * 512, 512, 0)
    second = lax.dynamic_slice_in_dim(out_weight, other * 512, 512, 0)
    plane = ("y", "xl", "xh", "z")
    got_first = move(first, plane, spread_target(0))
    got_second = move(second, plane, spread_target(1))
    got_first, got_second, mine = lax.optimization_barrier((got_first, got_second, mine))
    for_partner = jnp.where(xl == 0, got_first, got_second)
    for_self = jnp.where(xl == 0, got_second, got_first)
    weight_partner = lax.all_gather(for_partner, ("y", "xl", "c")).reshape(8, 2, 512, 512)
    weight_self = lax.all_gather(for_self, ("y", "xl", "c")).reshape(8, 2, 512, 512)

    theirs = swap_cores(mine)
    slots = jnp.concatenate([mine[:, 1024:1028, 0].reshape(32), theirs[:, 1024:1028, 0].reshape(32)])
    kv = sorted_kv(slots.astype(jnp.int32), mine, theirs)
    pieces = []
    for i in range(4):
        if i > 0:
            (queries,) = later(piece, queries)
        if i > 1:
            (queries,) = later(pieces[4 * i - 7 : 4 * i - 4], queries)
        piece = attention(i, own, order, queries, kv)
        pieces += [piece] + [move(piece, ("z",), lambda a, dz=dz: (a - dz,)) for dz in (1, 2, 3)]
    partner_sum, rows = partner_terms(order, pieces, weight_partner)
    got_sum = move(partner_sum, ("xh",), lambda a: (a + 1,))
    return own_terms(rows, weight_self, got_sum)


def solution(mesh):
    split = Mesh(mesh.devices.reshape([SIZES[a] for a in AXES]), AXES)
    seq, head = ("y", "xl", "c"), ("xh", "z")
    placed = (P(seq, head), P(seq, head), P(seq, head), P(seq), P(head, seq))
    return jax.shard_map(
        per_device, mesh=split, in_specs=placed, out_specs=P(seq, head), check_vma=False
    )
```

```python
import functools
import math

import jax
import jax.numpy as jnp
from jax import lax
from jax.experimental import pallas as pl
from jax.experimental.pallas import tpu as pltpu
from jax.sharding import Mesh
from jax.sharding import PartitionSpec as P

HD = 128
BLK = 128
TILE = 512
AXES = ("y", "xl", "c", "xh", "z")
SIZES = {"y": 4, "xl": 2, "c": 2, "xh": 2, "z": 4}
masked_score = -1e30
VMEM_BYTES = 56 << 20


def move(block, axes, target):
    sizes = [SIZES[a] for a in axes]
    count = math.prod(sizes)
    route = []
    for i in range(count):
        rest, at = i, []
        for size in reversed(sizes):
            at.append(rest % size)
            rest //= size
        to = target(*reversed(at))
        j = 0
        for t, size in zip(to, sizes):
            j = j * size + t % size
        route.append((i, j))
    return lax.ppermute(block, axes, route)


def run_all(copies):
    for copy in copies:
        copy.start()
    for copy in copies:
        copy.wait()


def sort_blocks(slot_ref, mine_ref, other_ref, sorted_ref, sem):
    run_all(
        [
            pltpu.make_async_copy(
                (mine_ref, other_ref)[i // 32].at[i // 4 % 8, pl.ds(i % 4 * 2 * BLK, 2 * BLK), :],
                sorted_ref.at[slot_ref[i]],
                sem.at[i],
            )
            for i in range(64)
        ]
    )


def sorted_kv(slots, mine, other):
    anywhere = pl.BlockSpec(memory_space=pl.ANY)
    return pl.pallas_call(
        sort_blocks,
        out_shape=jax.ShapeDtypeStruct((64, 2 * BLK, HD), jnp.bfloat16),
        in_specs=[pl.BlockSpec(memory_space=pltpu.SMEM), anywhere, anywhere],
        out_specs=pl.BlockSpec(memory_space=pltpu.VMEM),
        scratch_shapes=[pltpu.SemaphoreType.DMA((64,))],
        compiler_params=pltpu.CompilerParams(vmem_limit_bytes=VMEM_BYTES),
        cost_estimate=pl.CostEstimate(flops=0, bytes_accessed=8 << 20, transcendentals=0),
        name="sort_blocks",
    )(slots, mine, other)


def attend(chunk, heads, own_ref, order_ref, q_ref, kv_ref, out_ref, kv_s, q_s, s_s, acc, best, total, sem):
    rows = heads * BLK
    tile = TILE * 8 // heads
    per_tile = tile // BLK
    factor = math.log2(math.e) / math.sqrt(HD)
    block = own_ref[order_ref[chunk]]
    tiles = block // per_tile + 1

    def copy_of(j):
        slots = pl.ds(j * per_tile, per_tile)
        return pltpu.make_async_copy(kv_ref.at[slots], kv_s.at[slots], sem.at[j])

    def begin(j, carry):
        copy_of(j).start()
        return carry

    lax.fori_loop(0, tiles, begin, 0)
    for h in range(heads):
        q_s[h * BLK : (h + 1) * BLK, :] = q_ref[:, h * HD : (h + 1) * HD]
    acc[...] = jnp.zeros_like(acc)
    best[...] = jnp.full_like(best, masked_score)
    total[...] = jnp.zeros_like(total)

    def score(j):
        return lax.dot_general(
            kv_s[pl.ds(j * per_tile, per_tile), :BLK, :].reshape(tile, HD),
            q_s[...],
            (((1,), (1,)), ((), ())),
            preferred_element_type=jnp.float32,
        )

    def absorb(j, scores):
        old = best[...]
        new = jnp.maximum(old, jnp.max(scores, axis=0, keepdims=True))
        weights = jnp.exp2((scores - new) * factor)
        shrink = jnp.exp2((old - new) * factor)
        total[...] = total[...] * shrink + jnp.sum(weights, axis=0, keepdims=True)
        best[...] = new
        acc[...] = acc[...] * shrink + lax.dot_general(
            kv_s[pl.ds(j * per_tile, per_tile), BLK:, :].reshape(tile, HD),
            weights.astype(jnp.bfloat16),
            (((0,), (0,)), ((), ())),
            preferred_element_type=jnp.float32,
        )

    copy_of(0).wait()
    s_s[0] = score(0)

    def full_tile(j, carry):
        copy_of(j + 1).wait()
        scores = s_s[j % 2]
        s_s[(j + 1) % 2] = score(j + 1)
        absorb(j, scores)
        return carry

    lax.fori_loop(0, tiles - 1, full_tile, 0)
    last = tiles - 1
    key_at = last * tile + lax.broadcasted_iota(jnp.int32, (tile, rows), 0)
    query_at = block * BLK + lax.broadcasted_iota(jnp.int32, (tile, rows), 1) % BLK
    absorb(last, jnp.where(key_at <= query_at, s_s[last % 2], masked_score))
    result = acc[...] / total[...]
    for h in range(heads):
        part = result[:, h * BLK : (h + 1) * BLK]
        out_ref[:, h * HD : (h + 1) * HD] = part.T.astype(jnp.bfloat16)


def attention(chunk, part, heads, own, order, queries, kv):
    rows = heads * BLK
    tile = TILE * 8 // heads
    return pl.pallas_call(
        functools.partial(attend, chunk, heads),
        out_shape=jax.ShapeDtypeStruct((BLK, heads * HD), jnp.bfloat16),
        grid_spec=pltpu.PrefetchScalarGridSpec(
            num_scalar_prefetch=2,
            grid=(1,),
            in_specs=[
                pl.BlockSpec((BLK, heads * HD), lambda i, own, order: (order[chunk], part)),
                pl.BlockSpec(memory_space=pl.ANY),
            ],
            out_specs=pl.BlockSpec((BLK, heads * HD), lambda i, own, order: (0, 0)),
            scratch_shapes=[
                pltpu.VMEM((64, 2 * BLK, HD), jnp.bfloat16),
                pltpu.VMEM((rows, HD), jnp.bfloat16),
                pltpu.VMEM((2, tile, rows), jnp.float32),
                pltpu.VMEM((HD, rows), jnp.float32),
                pltpu.VMEM((1, rows), jnp.float32),
                pltpu.VMEM((1, rows), jnp.float32),
                pltpu.SemaphoreType.DMA((64 * BLK // tile,)),
            ],
        ),
        compiler_params=pltpu.CompilerParams(vmem_limit_bytes=VMEM_BYTES),
        cost_estimate=pl.CostEstimate(
            flops=1_250_000_000 * heads, bytes_accessed=1 << 22, transcendentals=0
        ),
        name="attend",
    )(own, order, queries, kv)


def project_partner(places, order_ref, *refs):
    pieces, (w_ref, out_ref, all_ref, a_s, sem) = refs[:-5], refs[-5:]
    n = pl.program_id(0)
    keep = pltpu.make_async_copy(a_s, all_ref, sem.at[len(pieces)])

    @pl.when(n == 0)
    def _():
        run_all(
            [
                pltpu.make_async_copy(
                    piece,
                    a_s.at[
                        pl.ds(pl.multiple_of(order_ref[chunk] * BLK, BLK), BLK),
                        pl.ds(at, piece.shape[1]),
                    ],
                    sem.at[i],
                )
                for i, (piece, (chunk, at)) in enumerate(zip(pieces, places))
            ]
        )
        keep.start()

    w = w_ref[...].reshape(4096, 256)
    out = jnp.dot(a_s[...], w, preferred_element_type=jnp.float32)
    out_ref[...] = out.astype(jnp.bfloat16)

    @pl.when(n == pl.num_programs(0) - 1)
    def _():
        keep.wait()


def partner_terms(order, pieces, places, weight):
    return pl.pallas_call(
        functools.partial(project_partner, places),
        out_shape=(
            jax.ShapeDtypeStruct((512, 512), jnp.bfloat16),
            jax.ShapeDtypeStruct((512, 4096), jnp.bfloat16),
        ),
        grid_spec=pltpu.PrefetchScalarGridSpec(
            num_scalar_prefetch=1,
            grid=(2,),
            in_specs=[pl.BlockSpec(memory_space=pl.ANY)] * len(pieces)
            + [pl.BlockSpec((8, None, 512, 256), lambda n, o: (0, 0, 0, n))],
            out_specs=(
                pl.BlockSpec((512, 256), lambda n, o: (0, n)),
                pl.BlockSpec(memory_space=pl.ANY),
            ),
            scratch_shapes=[
                pltpu.VMEM((512, 4096), jnp.bfloat16),
                pltpu.SemaphoreType.DMA((len(pieces) + 1,)),
            ],
        ),
        compiler_params=pltpu.CompilerParams(vmem_limit_bytes=VMEM_BYTES),
        cost_estimate=pl.CostEstimate(
            flops=2 * 512 * 4096 * 512, bytes_accessed=14 << 20, transcendentals=0
        ),
        name="project_partner",
    )(order, *pieces, weight)


def project_rest(a_ref, w_ref, out_ref):
    w = w_ref[...].reshape(4096, 256)
    out = jnp.dot(a_ref[...], w, preferred_element_type=jnp.float32)
    out_ref[...] = out.astype(jnp.bfloat16)


def rest_terms(rows, weight):
    return pl.pallas_call(
        project_rest,
        out_shape=jax.ShapeDtypeStruct((512, 512), jnp.bfloat16),
        grid=(2,),
        in_specs=[
            pl.BlockSpec((512, 4096), lambda n: (0, 0)),
            pl.BlockSpec((8, None, 512, 256), lambda n: (0, 1, 0, n)),
        ],
        out_specs=pl.BlockSpec((512, 256), lambda n: (0, n)),
        compiler_params=pltpu.CompilerParams(vmem_limit_bytes=VMEM_BYTES),
        cost_estimate=pl.CostEstimate(
            flops=2 * 512 * 4096 * 512, bytes_accessed=9 << 20, transcendentals=0
        ),
        name="project_rest",
    )(rows, weight)


def project_self(a_ref, w_ref, first_ref, second_ref, out_ref):
    w = w_ref[...].reshape(4096, 256)
    out = jnp.dot(a_ref[...], w, preferred_element_type=jnp.float32)
    other = jnp.where(pl.program_id(0) < 2, first_ref[...], second_ref[...])
    out_ref[...] = (out + other.astype(jnp.float32)).astype(jnp.bfloat16)


def own_terms(rows, weight, first, second):
    return pl.pallas_call(
        project_self,
        out_shape=jax.ShapeDtypeStruct((512, 1024), jnp.bfloat16),
        grid=(4,),
        in_specs=[
            pl.BlockSpec((512, 4096), lambda n: (0, 0)),
            pl.BlockSpec((8, None, 512, 256), lambda n: (0, n // 2, 0, n % 2)),
            pl.BlockSpec((512, 256), lambda n: (0, jnp.minimum(n, 1))),
            pl.BlockSpec((512, 256), lambda n: (0, jnp.maximum(n - 2, 0))),
        ],
        out_specs=pl.BlockSpec((512, 256), lambda n: (0, n)),
        compiler_params=pltpu.CompilerParams(vmem_limit_bytes=VMEM_BYTES),
        cost_estimate=pl.CostEstimate(
            flops=2 * 512 * 4096 * 1024, bytes_accessed=14 << 20, transcendentals=0
        ),
        name="project_self",
    )(rows, weight, first, second)


def spread_target(half):
    def target(y, xl, xh, z):
        plane = (y % 2) * 2 + xl
        other = (y // 2) ^ xh
        part = half if other else 1 - half
        return ((z - plane) % 4, part, xh, plane)

    return target


def swap_cores(block):
    return move(block, ("c",), lambda a: (a + 1,))


def per_device(queries, keys, values, positions, out_weight):
    y, xl, xh = lax.axis_index("y"), lax.axis_index("xl"), lax.axis_index("xh")
    own = positions[::BLK] // BLK
    index = jnp.arange(4, dtype=jnp.int32)
    rank = jnp.sum((own[None, :] < own[:, None]).astype(jnp.int32), axis=1)
    order = jnp.sum(jnp.where(rank[None, :] == index[:, None], index[None, :], 0), axis=1)
    ids = jnp.broadcast_to(own.astype(jnp.bfloat16)[None, :, None], (4, 4, HD)).reshape(16, HD)
    pairs = jnp.stack([keys.reshape(4, BLK, HD), values.reshape(4, BLK, HD)], 1)
    packet = jnp.concatenate([pairs.reshape(8 * BLK, HD), ids])
    copies = jnp.broadcast_to(packet[None], (8, *packet.shape))
    mine = lax.all_to_all(copies, ("y", "xl"), 0, 0, tiled=True)

    def later(first, *values):
        return lax.optimization_barrier((first, *values))[1:]

    other = (y // 2) ^ xh
    first = lax.dynamic_slice_in_dim(out_weight, (1 - other) * 512, 512, 0)
    second = lax.dynamic_slice_in_dim(out_weight, other * 512, 512, 0)
    plane = ("y", "xl", "xh", "z")
    got_first = move(first, plane, spread_target(0))
    got_second = move(second, plane, spread_target(1))
    got_first, got_second, mine = lax.optimization_barrier((got_first, got_second, mine))
    for_partner = jnp.where(xl == 0, got_first, got_second)
    for_self = jnp.where(xl == 0, got_second, got_first)
    weight_partner = lax.all_gather(for_partner, ("y", "xl", "c")).reshape(8, 2, 512, 512)
    weight_self = lax.all_gather(for_self, ("y", "xl", "c")).reshape(8, 2, 512, 512)

    theirs = swap_cores(mine)
    slots = jnp.concatenate([mine[:, 1024:1028, 0].reshape(32), theirs[:, 1024:1028, 0].reshape(32)])
    kv = sorted_kv(slots.astype(jnp.int32), mine, theirs)
    sets, places = [], []
    for chunk, part, heads in ((0, 0, 8), (1, 0, 8), (2, 0, 8), (3, 0, 4), (3, 1, 4)):
        if sets:
            (queries,) = later(sets[-1][0], queries)
        if len(sets) > 1:
            (queries,) = later(sets[-2][1:], queries)
        piece = attention(chunk, part, heads, own, order, queries, kv)
        around = [move(piece, ("z",), lambda a, dz=dz: (a - dz,)) for dz in (1, 2, 3)]
        sets.append([piece] + around)
        places += [(chunk, dz * 1024 + part * 512) for dz in range(4)]
    pieces = [piece for group in sets for piece in group]
    first_sum, rows = partner_terms(order, pieces, tuple(places), weight_partner)
    got_first = move(first_sum, ("xh",), lambda a: (a + 1,))
    second_sum = rest_terms(rows, weight_partner)
    got_second = move(second_sum, ("xh",), lambda a: (a + 1,))
    return own_terms(rows, weight_self, got_first, got_second)


def solution(mesh):
    split = Mesh(mesh.devices.reshape([SIZES[a] for a in AXES]), AXES)
    seq, head = ("y", "xl", "c"), ("xh", "z")
    placed = (P(seq, head), P(seq, head), P(seq, head), P(seq), P(head, seq))
    return jax.shard_map(
        per_device, mesh=split, in_specs=placed, out_specs=P(seq, head), check_vma=False
    )
```

```python
import functools
import math

import jax
import jax.numpy as jnp
from jax import lax
from jax.experimental import pallas as pl
from jax.experimental.pallas import tpu as pltpu
from jax.sharding import Mesh
from jax.sharding import PartitionSpec as P

HD = 128
BLK = 128
TILE = 512
AXES = ("y", "xl", "c", "xh", "z")
SIZES = {"y": 4, "xl": 2, "c": 2, "xh": 2, "z": 4}
masked_score = -1e30
VMEM_BYTES = 56 << 20


def move(block, axes, target):
    sizes = [SIZES[a] for a in axes]
    count = math.prod(sizes)
    route = []
    for i in range(count):
        rest, at = i, []
        for size in reversed(sizes):
            at.append(rest % size)
            rest //= size
        to = target(*reversed(at))
        j = 0
        for t, size in zip(to, sizes):
            j = j * size + t % size
        route.append((i, j))
    return lax.ppermute(block, axes, route)


def run_all(copies):
    for copy in copies:
        copy.start()
    for copy in copies:
        copy.wait()


def sort_blocks(slot_ref, mine_ref, other_ref, sorted_ref, sem):
    run_all(
        [
            pltpu.make_async_copy(
                (mine_ref, other_ref)[i // 32].at[i // 4 % 8, pl.ds(i % 4 * 2 * BLK, 2 * BLK), :],
                sorted_ref.at[slot_ref[i]],
                sem.at[i],
            )
            for i in range(64)
        ]
    )


def sorted_kv(slots, mine, other):
    anywhere = pl.BlockSpec(memory_space=pl.ANY)
    return pl.pallas_call(
        sort_blocks,
        out_shape=jax.ShapeDtypeStruct((64, 2 * BLK, HD), jnp.bfloat16),
        in_specs=[pl.BlockSpec(memory_space=pltpu.SMEM), anywhere, anywhere],
        out_specs=pl.BlockSpec(memory_space=pltpu.VMEM),
        scratch_shapes=[pltpu.SemaphoreType.DMA((64,))],
        compiler_params=pltpu.CompilerParams(vmem_limit_bytes=VMEM_BYTES),
        cost_estimate=pl.CostEstimate(flops=0, bytes_accessed=8 << 20, transcendentals=0),
        name="sort_blocks",
    )(slots, mine, other)


def attend(chunk, heads, own_ref, order_ref, q_ref, kv_ref, out_ref, kv_s, q_s, s_s, acc, best, total, sem):
    rows = heads * BLK
    tile = TILE * 8 // heads
    per_tile = tile // BLK
    factor = math.log2(math.e) / math.sqrt(HD)
    block = own_ref[order_ref[chunk]]
    tiles = block // per_tile + 1

    def copy_of(j):
        slots = pl.ds(j * per_tile, per_tile)
        return pltpu.make_async_copy(kv_ref.at[slots], kv_s.at[slots], sem.at[j])

    def begin(j, carry):
        copy_of(j).start()
        return carry

    lax.fori_loop(0, tiles, begin, 0)
    for h in range(heads):
        q_s[h * BLK : (h + 1) * BLK, :] = q_ref[:, h * HD : (h + 1) * HD]
    acc[...] = jnp.zeros_like(acc)
    best[...] = jnp.full_like(best, masked_score)
    total[...] = jnp.zeros_like(total)

    def score(j):
        return lax.dot_general(
            kv_s[pl.ds(j * per_tile, per_tile), :BLK, :].reshape(tile, HD),
            q_s[...],
            (((1,), (1,)), ((), ())),
            preferred_element_type=jnp.float32,
        )

    def absorb(j, scores):
        old = best[...]
        new = jnp.maximum(old, jnp.max(scores, axis=0, keepdims=True))
        weights = jnp.exp2((scores - new) * factor)
        shrink = jnp.exp2((old - new) * factor)
        total[...] = total[...] * shrink + jnp.sum(weights, axis=0, keepdims=True)
        best[...] = new
        acc[...] = acc[...] * shrink + lax.dot_general(
            kv_s[pl.ds(j * per_tile, per_tile), BLK:, :].reshape(tile, HD),
            weights.astype(jnp.bfloat16),
            (((0,), (0,)), ((), ())),
            preferred_element_type=jnp.float32,
        )

    copy_of(0).wait()
    s_s[0] = score(0)

    def full_tile(j, carry):
        copy_of(j + 1).wait()
        scores = s_s[j % 2]
        s_s[(j + 1) % 2] = score(j + 1)
        absorb(j, scores)
        return carry

    lax.fori_loop(0, tiles - 1, full_tile, 0)
    last = tiles - 1
    key_at = last * tile + lax.broadcasted_iota(jnp.int32, (tile, rows), 0)
    query_at = block * BLK + lax.broadcasted_iota(jnp.int32, (tile, rows), 1) % BLK
    absorb(last, jnp.where(key_at <= query_at, s_s[last % 2], masked_score))
    result = acc[...] / total[...]
    for h in range(heads):
        part = result[:, h * BLK : (h + 1) * BLK]
        out_ref[:, h * HD : (h + 1) * HD] = part.T.astype(jnp.bfloat16)


def attention(chunk, part, heads, own, order, queries, kv):
    rows = heads * BLK
    tile = TILE * 8 // heads
    return pl.pallas_call(
        functools.partial(attend, chunk, heads),
        out_shape=jax.ShapeDtypeStruct((BLK, heads * HD), jnp.bfloat16),
        grid_spec=pltpu.PrefetchScalarGridSpec(
            num_scalar_prefetch=2,
            grid=(1,),
            in_specs=[
                pl.BlockSpec((BLK, heads * HD), lambda i, own, order: (order[chunk], part)),
                pl.BlockSpec(memory_space=pl.ANY),
            ],
            out_specs=pl.BlockSpec((BLK, heads * HD), lambda i, own, order: (0, 0)),
            scratch_shapes=[
                pltpu.VMEM((64, 2 * BLK, HD), jnp.bfloat16),
                pltpu.VMEM((rows, HD), jnp.bfloat16),
                pltpu.VMEM((2, tile, rows), jnp.float32),
                pltpu.VMEM((HD, rows), jnp.float32),
                pltpu.VMEM((1, rows), jnp.float32),
                pltpu.VMEM((1, rows), jnp.float32),
                pltpu.SemaphoreType.DMA((64 * BLK // tile,)),
            ],
        ),
        compiler_params=pltpu.CompilerParams(vmem_limit_bytes=VMEM_BYTES),
        cost_estimate=pl.CostEstimate(
            flops=1_250_000_000 * heads, bytes_accessed=1 << 22, transcendentals=0
        ),
        name="attend",
    )(own, order, queries, kv)


def project_partner(places, order_ref, *refs):
    pieces, (w_ref, out_ref, all_ref, a_s, sem) = refs[:-5], refs[-5:]
    n = pl.program_id(0)
    keep = pltpu.make_async_copy(a_s, all_ref, sem.at[len(pieces)])

    @pl.when(n == 0)
    def _():
        run_all(
            [
                pltpu.make_async_copy(
                    piece,
                    a_s.at[
                        pl.ds(pl.multiple_of(order_ref[chunk] * BLK, BLK), BLK),
                        pl.ds(at, piece.shape[1]),
                    ],
                    sem.at[i],
                )
                for i, (piece, (chunk, at)) in enumerate(zip(pieces, places))
            ]
        )
        keep.start()

    w = w_ref[...].reshape(4096, 256)
    out = jnp.dot(a_s[...], w, preferred_element_type=jnp.float32)
    out_ref[...] = out.astype(jnp.bfloat16)

    @pl.when(n == pl.num_programs(0) - 1)
    def _():
        keep.wait()


def partner_terms(order, pieces, places, weight):
    return pl.pallas_call(
        functools.partial(project_partner, places),
        out_shape=(
            jax.ShapeDtypeStruct((512, 512), jnp.bfloat16),
            jax.ShapeDtypeStruct((512, 4096), jnp.bfloat16),
        ),
        grid_spec=pltpu.PrefetchScalarGridSpec(
            num_scalar_prefetch=1,
            grid=(2,),
            in_specs=[pl.BlockSpec(memory_space=pl.ANY)] * len(pieces)
            + [pl.BlockSpec((8, None, 512, 256), lambda n, o: (0, 0, 0, n))],
            out_specs=(
                pl.BlockSpec((512, 256), lambda n, o: (0, n)),
                pl.BlockSpec(memory_space=pl.ANY),
            ),
            scratch_shapes=[
                pltpu.VMEM((512, 4096), jnp.bfloat16),
                pltpu.SemaphoreType.DMA((len(pieces) + 1,)),
            ],
        ),
        compiler_params=pltpu.CompilerParams(vmem_limit_bytes=VMEM_BYTES),
        cost_estimate=pl.CostEstimate(
            flops=2 * 512 * 4096 * 512, bytes_accessed=14 << 20, transcendentals=0
        ),
        name="project_partner",
    )(order, *pieces, weight)


def project_rest(a_ref, w_ref, out_ref):
    w = w_ref[...].reshape(4096, 256)
    out = jnp.dot(a_ref[...], w, preferred_element_type=jnp.float32)
    out_ref[...] = out.astype(jnp.bfloat16)


def rest_terms(rows, weight):
    return pl.pallas_call(
        project_rest,
        out_shape=jax.ShapeDtypeStruct((512, 512), jnp.bfloat16),
        grid=(2,),
        in_specs=[
            pl.BlockSpec((512, 4096), lambda n: (0, 0)),
            pl.BlockSpec((8, None, 512, 256), lambda n: (0, 1, 0, n)),
        ],
        out_specs=pl.BlockSpec((512, 256), lambda n: (0, n)),
        compiler_params=pltpu.CompilerParams(vmem_limit_bytes=VMEM_BYTES),
        cost_estimate=pl.CostEstimate(
            flops=2 * 512 * 4096 * 512, bytes_accessed=9 << 20, transcendentals=0
        ),
        name="project_rest",
    )(rows, weight)


def project_self(a_ref, w_ref, first_ref, second_ref, out_ref):
    w = w_ref[...].reshape(4096, 256)
    out = jnp.dot(a_ref[...], w, preferred_element_type=jnp.float32)
    other = jnp.where(pl.program_id(0) < 2, first_ref[...], second_ref[...])
    out_ref[...] = (out + other.astype(jnp.float32)).astype(jnp.bfloat16)


def own_terms(rows, weight, first, second):
    return pl.pallas_call(
        project_self,
        out_shape=jax.ShapeDtypeStruct((512, 1024), jnp.bfloat16),
        grid=(4,),
        in_specs=[
            pl.BlockSpec((512, 4096), lambda n: (0, 0)),
            pl.BlockSpec((8, None, 512, 256), lambda n: (0, n // 2, 0, n % 2)),
            pl.BlockSpec((512, 256), lambda n: (0, jnp.minimum(n, 1))),
            pl.BlockSpec((512, 256), lambda n: (0, jnp.maximum(n - 2, 0))),
        ],
        out_specs=pl.BlockSpec((512, 256), lambda n: (0, n)),
        compiler_params=pltpu.CompilerParams(vmem_limit_bytes=VMEM_BYTES),
        cost_estimate=pl.CostEstimate(
            flops=2 * 512 * 4096 * 1024, bytes_accessed=14 << 20, transcendentals=0
        ),
        name="project_self",
    )(rows, weight, first, second)


def spread_target(half):
    def target(y, xl, xh, z):
        plane = (y % 2) * 2 + xl
        other = (y // 2) ^ xh
        part = half if other else 1 - half
        return ((z - plane) % 4, part, xh, plane)

    return target


def swap_cores(block):
    return move(block, ("c",), lambda a: (a + 1,))


def per_device(queries, keys, values, positions, out_weight):
    y, xl, xh = lax.axis_index("y"), lax.axis_index("xl"), lax.axis_index("xh")
    own = positions[::BLK] // BLK
    index = jnp.arange(4, dtype=jnp.int32)
    rank = jnp.sum((own[None, :] < own[:, None]).astype(jnp.int32), axis=1)
    order = jnp.sum(jnp.where(rank[None, :] == index[:, None], index[None, :], 0), axis=1)
    ids = jnp.broadcast_to(own.astype(jnp.bfloat16)[None, :, None], (4, 4, HD)).reshape(16, HD)
    pairs = jnp.stack([keys.reshape(4, BLK, HD), values.reshape(4, BLK, HD)], 1)
    packet = jnp.concatenate([pairs.reshape(8 * BLK, HD), ids])
    copies = jnp.broadcast_to(packet[None], (8, *packet.shape))
    mine = lax.all_to_all(copies, ("y", "xl"), 0, 0, tiled=True)

    def later(first, *values):
        return lax.optimization_barrier((first, *values))[1:]

    (out_weight,) = later(mine, out_weight)
    other = (y // 2) ^ xh
    first = lax.dynamic_slice_in_dim(out_weight, (1 - other) * 512, 512, 0)
    second = lax.dynamic_slice_in_dim(out_weight, other * 512, 512, 0)
    plane = ("y", "xl", "xh", "z")
    got_first = move(first, plane, spread_target(0))
    got_second = move(second, plane, spread_target(1))
    theirs = swap_cores(mine)
    slots = jnp.concatenate([mine[:, 1024:1028, 0].reshape(32), theirs[:, 1024:1028, 0].reshape(32)])
    kv = sorted_kv(slots.astype(jnp.int32), mine, theirs)
    sets, places = [], []
    for chunk, part, heads in ((0, 0, 8), (1, 0, 8), (2, 0, 8), (3, 0, 4), (3, 1, 4)):
        if sets:
            (queries,) = later(sets[-1][0], queries)
        if len(sets) > 1:
            (queries,) = later(sets[-2][1:], queries)
        piece = attention(chunk, part, heads, own, order, queries, kv)
        around = [move(piece, ("z",), lambda a, dz=dz: (a - dz,)) for dz in (1, 2, 3)]
        sets.append([piece] + around)
        if chunk == 0:
            got_first, got_second = later(piece, got_first, got_second)
            for_partner = jnp.where(xl == 0, got_first, got_second)
            for_self = jnp.where(xl == 0, got_second, got_first)
            weight_partner = lax.all_gather(for_partner, ("y", "xl", "c")).reshape(8, 2, 512, 512)
            weight_self = lax.all_gather(for_self, ("y", "xl", "c")).reshape(8, 2, 512, 512)
        places += [(chunk, dz * 1024 + part * 512) for dz in range(4)]
    pieces = [piece for group in sets for piece in group]
    first_sum, rows = partner_terms(order, pieces, tuple(places), weight_partner)
    got_first = move(first_sum, ("xh",), lambda a: (a + 1,))
    second_sum = rest_terms(rows, weight_partner)
    got_second = move(second_sum, ("xh",), lambda a: (a + 1,))
    return own_terms(rows, weight_self, got_first, got_second)


def solution(mesh):
    split = Mesh(mesh.devices.reshape([SIZES[a] for a in AXES]), AXES)
    seq, head = ("y", "xl", "c"), ("xh", "z")
    placed = (P(seq, head), P(seq, head), P(seq, head), P(seq), P(head, seq))
    return jax.shard_map(
        per_device, mesh=split, in_specs=placed, out_specs=P(seq, head), check_vma=False
    )
```

```python
import functools
import math

import jax
import jax.numpy as jnp
from jax import lax
from jax.experimental import pallas as pl
from jax.experimental.pallas import tpu as pltpu
from jax.sharding import Mesh
from jax.sharding import PartitionSpec as P

HD = 128
BLK = 128
TILE = 512
AXES = ("y", "xl", "c", "xh", "z")
SIZES = {"y": 4, "xl": 2, "c": 2, "xh": 2, "z": 4}
masked_score = -1e30
VMEM_BYTES = 56 << 20


def move(block, axes, target):
    sizes = [SIZES[a] for a in axes]
    count = math.prod(sizes)
    route = []
    for i in range(count):
        rest, at = i, []
        for size in reversed(sizes):
            at.append(rest % size)
            rest //= size
        to = target(*reversed(at))
        j = 0
        for t, size in zip(to, sizes):
            j = j * size + t % size
        route.append((i, j))
    return lax.ppermute(block, axes, route)


def run_all(copies):
    for copy in copies:
        copy.start()
    for copy in copies:
        copy.wait()


def sort_blocks(slot_ref, mine_ref, other_ref, sorted_ref, sem):
    run_all(
        [
            pltpu.make_async_copy(
                (mine_ref, other_ref)[i // 32].at[i // 4 % 8, pl.ds(i % 4 * 2 * BLK, 2 * BLK), :],
                sorted_ref.at[slot_ref[i]],
                sem.at[i],
            )
            for i in range(64)
        ]
    )


def sorted_kv(slots, mine, other):
    anywhere = pl.BlockSpec(memory_space=pl.ANY)
    return pl.pallas_call(
        sort_blocks,
        out_shape=jax.ShapeDtypeStruct((64, 2 * BLK, HD), jnp.bfloat16),
        in_specs=[pl.BlockSpec(memory_space=pltpu.SMEM), anywhere, anywhere],
        out_specs=pl.BlockSpec(memory_space=pltpu.VMEM),
        scratch_shapes=[pltpu.SemaphoreType.DMA((64,))],
        compiler_params=pltpu.CompilerParams(vmem_limit_bytes=VMEM_BYTES),
        cost_estimate=pl.CostEstimate(flops=0, bytes_accessed=8 << 20, transcendentals=0),
        name="sort_blocks",
    )(slots, mine, other)


def attend(chunk, heads, own_ref, order_ref, q_ref, kv_ref, out_ref, kv_s, q_s, s_s, acc, best, total, sem):
    rows = heads * BLK
    tile = TILE * 8 // heads
    per_tile = tile // BLK
    factor = math.log2(math.e) / math.sqrt(HD)
    block = own_ref[order_ref[chunk]]
    tiles = block // per_tile + 1

    def copy_of(j):
        slots = pl.ds(j * per_tile, per_tile)
        return pltpu.make_async_copy(kv_ref.at[slots], kv_s.at[slots], sem.at[j])

    def begin(j, carry):
        copy_of(j).start()
        return carry

    lax.fori_loop(0, tiles, begin, 0)
    for h in range(heads):
        q_s[h * BLK : (h + 1) * BLK, :] = q_ref[:, h * HD : (h + 1) * HD]
    acc[...] = jnp.zeros_like(acc)
    best[...] = jnp.full_like(best, masked_score)
    total[...] = jnp.zeros_like(total)

    def score(j):
        return lax.dot_general(
            kv_s[pl.ds(j * per_tile, per_tile), :BLK, :].reshape(tile, HD),
            q_s[...],
            (((1,), (1,)), ((), ())),
            preferred_element_type=jnp.float32,
        )

    def absorb(j, scores):
        old = best[...]
        new = jnp.maximum(old, jnp.max(scores, axis=0, keepdims=True))
        weights = jnp.exp2((scores - new) * factor)
        shrink = jnp.exp2((old - new) * factor)
        total[...] = total[...] * shrink + jnp.sum(weights, axis=0, keepdims=True)
        best[...] = new
        acc[...] = acc[...] * shrink + lax.dot_general(
            kv_s[pl.ds(j * per_tile, per_tile), BLK:, :].reshape(tile, HD),
            weights.astype(jnp.bfloat16),
            (((0,), (0,)), ((), ())),
            preferred_element_type=jnp.float32,
        )

    copy_of(0).wait()
    s_s[0] = score(0)

    def full_tile(j, carry):
        copy_of(j + 1).wait()
        scores = s_s[j % 2]
        s_s[(j + 1) % 2] = score(j + 1)
        absorb(j, scores)
        return carry

    lax.fori_loop(0, tiles - 1, full_tile, 0)
    last = tiles - 1
    key_at = last * tile + lax.broadcasted_iota(jnp.int32, (tile, rows), 0)
    query_at = block * BLK + lax.broadcasted_iota(jnp.int32, (tile, rows), 1) % BLK
    absorb(last, jnp.where(key_at <= query_at, s_s[last % 2], masked_score))
    result = acc[...] / total[...]
    for h in range(heads):
        part = result[:, h * BLK : (h + 1) * BLK]
        out_ref[:, h * HD : (h + 1) * HD] = part.T.astype(jnp.bfloat16)


def attention(chunk, part, heads, own, order, queries, kv):
    rows = heads * BLK
    tile = TILE * 8 // heads
    return pl.pallas_call(
        functools.partial(attend, chunk, heads),
        out_shape=jax.ShapeDtypeStruct((BLK, heads * HD), jnp.bfloat16),
        grid_spec=pltpu.PrefetchScalarGridSpec(
            num_scalar_prefetch=2,
            grid=(1,),
            in_specs=[
                pl.BlockSpec((BLK, heads * HD), lambda i, own, order: (order[chunk], part)),
                pl.BlockSpec(memory_space=pl.ANY),
            ],
            out_specs=pl.BlockSpec((BLK, heads * HD), lambda i, own, order: (0, 0)),
            scratch_shapes=[
                pltpu.VMEM((64, 2 * BLK, HD), jnp.bfloat16),
                pltpu.VMEM((rows, HD), jnp.bfloat16),
                pltpu.VMEM((2, tile, rows), jnp.float32),
                pltpu.VMEM((HD, rows), jnp.float32),
                pltpu.VMEM((1, rows), jnp.float32),
                pltpu.VMEM((1, rows), jnp.float32),
                pltpu.SemaphoreType.DMA((64 * BLK // tile,)),
            ],
        ),
        compiler_params=pltpu.CompilerParams(vmem_limit_bytes=VMEM_BYTES),
        cost_estimate=pl.CostEstimate(
            flops=1_250_000_000 * heads, bytes_accessed=1 << 22, transcendentals=0
        ),
        name="attend",
    )(own, order, queries, kv)


def project_partner(places, order_ref, *refs):
    pieces, (w_ref, out_ref, all_ref, a_s, sem) = refs[:-5], refs[-5:]
    n = pl.program_id(0)
    keep = pltpu.make_async_copy(a_s, all_ref, sem.at[len(pieces)])

    @pl.when(n == 0)
    def _():
        run_all(
            [
                pltpu.make_async_copy(
                    piece,
                    a_s.at[
                        pl.ds(pl.multiple_of(order_ref[chunk] * BLK, BLK), BLK),
                        pl.ds(at, piece.shape[1]),
                    ],
                    sem.at[i],
                )
                for i, (piece, (chunk, at)) in enumerate(zip(pieces, places))
            ]
        )
        keep.start()

    w = w_ref[...].reshape(4096, 256)
    out = jnp.dot(a_s[...], w, preferred_element_type=jnp.float32)
    out_ref[...] = out.astype(jnp.bfloat16)

    @pl.when(n == pl.num_programs(0) - 1)
    def _():
        keep.wait()


def partner_terms(order, pieces, places, weight):
    return pl.pallas_call(
        functools.partial(project_partner, places),
        out_shape=(
            jax.ShapeDtypeStruct((512, 512), jnp.bfloat16),
            jax.ShapeDtypeStruct((512, 4096), jnp.bfloat16),
        ),
        grid_spec=pltpu.PrefetchScalarGridSpec(
            num_scalar_prefetch=1,
            grid=(2,),
            in_specs=[pl.BlockSpec(memory_space=pl.ANY)] * len(pieces)
            + [pl.BlockSpec((8, None, None, 512, 256), lambda n, o: (0, 0, 0, 0, n))],
            out_specs=(
                pl.BlockSpec((512, 256), lambda n, o: (0, n)),
                pl.BlockSpec(memory_space=pl.ANY),
            ),
            scratch_shapes=[
                pltpu.VMEM((512, 4096), jnp.bfloat16),
                pltpu.SemaphoreType.DMA((len(pieces) + 1,)),
            ],
        ),
        compiler_params=pltpu.CompilerParams(vmem_limit_bytes=VMEM_BYTES),
        cost_estimate=pl.CostEstimate(
            flops=2 * 512 * 4096 * 512, bytes_accessed=14 << 20, transcendentals=0
        ),
        name="project_partner",
    )(order, *pieces, weight)


def project_rest(a_ref, w_ref, out_ref):
    w = w_ref[...].reshape(4096, 256)
    out = jnp.dot(a_ref[...], w, preferred_element_type=jnp.float32)
    out_ref[...] = out.astype(jnp.bfloat16)


def rest_terms(rows, weight):
    return pl.pallas_call(
        project_rest,
        out_shape=jax.ShapeDtypeStruct((512, 512), jnp.bfloat16),
        grid=(2,),
        in_specs=[
            pl.BlockSpec((512, 4096), lambda n: (0, 0)),
            pl.BlockSpec((8, None, None, 512, 256), lambda n: (0, 1, 0, 0, n)),
        ],
        out_specs=pl.BlockSpec((512, 256), lambda n: (0, n)),
        compiler_params=pltpu.CompilerParams(vmem_limit_bytes=VMEM_BYTES),
        cost_estimate=pl.CostEstimate(
            flops=2 * 512 * 4096 * 512, bytes_accessed=9 << 20, transcendentals=0
        ),
        name="project_rest",
    )(rows, weight)


def project_self(a_ref, w_ref, out_ref):
    w = w_ref[...].reshape(4096, 256)
    out_ref[...] = jnp.dot(a_ref[...], w, preferred_element_type=jnp.float32)


def own_terms(rows, weight):
    return pl.pallas_call(
        project_self,
        out_shape=jax.ShapeDtypeStruct((512, 1024), jnp.float32),
        grid=(4,),
        in_specs=[
            pl.BlockSpec((512, 4096), lambda n: (0, 0)),
            pl.BlockSpec((8, None, None, 512, 256), lambda n: (0, n // 2, 1, 0, n % 2)),
        ],
        out_specs=pl.BlockSpec((512, 256), lambda n: (0, n)),
        compiler_params=pltpu.CompilerParams(vmem_limit_bytes=VMEM_BYTES),
        cost_estimate=pl.CostEstimate(
            flops=2 * 512 * 4096 * 1024, bytes_accessed=14 << 20, transcendentals=0
        ),
        name="project_self",
    )(rows, weight)


def spread_target(half):
    def target(y, xl, xh, z):
        plane = (y % 2) * 2 + xl
        other = (y // 2) ^ xh
        part = half if other else 1 - half
        return ((z - plane) % 4, part, xh, plane)

    return target


def swap_cores(block):
    return move(block, ("c",), lambda a: (a + 1,))


def per_device(queries, keys, values, positions, out_weight):
    y, xl, xh = lax.axis_index("y"), lax.axis_index("xl"), lax.axis_index("xh")
    own = positions[::BLK] // BLK
    index = jnp.arange(4, dtype=jnp.int32)
    rank = jnp.sum((own[None, :] < own[:, None]).astype(jnp.int32), axis=1)
    order = jnp.sum(jnp.where(rank[None, :] == index[:, None], index[None, :], 0), axis=1)
    ids = jnp.broadcast_to(own.astype(jnp.bfloat16)[None, :, None], (4, 4, HD)).reshape(16, HD)
    pairs = jnp.stack([keys.reshape(4, BLK, HD), values.reshape(4, BLK, HD)], 1)
    packet = jnp.concatenate([pairs.reshape(8 * BLK, HD), ids])
    copies = jnp.broadcast_to(packet[None], (8, *packet.shape))
    mine = lax.all_to_all(copies, ("y", "xl"), 0, 0, tiled=True)

    def later(first, *values):
        return lax.optimization_barrier((first, *values))[1:]

    other = (y // 2) ^ xh
    first = lax.dynamic_slice_in_dim(out_weight, (1 - other) * 512, 512, 0)
    second = lax.dynamic_slice_in_dim(out_weight, other * 512, 512, 0)
    plane = ("y", "xl", "xh", "z")
    got_first = move(first, plane, spread_target(0))
    got_second = move(second, plane, spread_target(1))
    got_first, got_second, mine = lax.optimization_barrier((got_first, got_second, mine))
    theirs = swap_cores(mine)
    both = jnp.where(xl == 0, jnp.stack([got_first, got_second]), jnp.stack([got_second, got_first]))
    weight = lax.all_gather(both.reshape(1024, 512), ("y", "xl", "c")).reshape(8, 2, 2, 512, 512)
    slots = jnp.concatenate([mine[:, 1024:1028, 0].reshape(32), theirs[:, 1024:1028, 0].reshape(32)])
    kv = sorted_kv(slots.astype(jnp.int32), mine, theirs)

    sets, places = [], []
    for chunk, part, heads in ((0, 0, 8), (1, 0, 8), (2, 0, 8), (3, 0, 4), (3, 1, 4)):
        if sets:
            (queries,) = later(sets[-1][0], queries)
        if len(sets) > 1:
            (queries,) = later(sets[-2][1:], queries)
        piece = attention(chunk, part, heads, own, order, queries, kv)
        around = [move(piece, ("z",), lambda a, dz=dz: (a - dz,)) for dz in (1, 2, 3)]
        sets.append([piece] + around)
        places += [(chunk, dz * 1024 + part * 512) for dz in range(4)]
    pieces = [piece for group in sets for piece in group]
    first_sum, rows = partner_terms(order, pieces, tuple(places), weight)
    got_first = move(first_sum, ("xh",), lambda a: (a + 1,))
    second_sum = rest_terms(rows, weight)
    got_second = move(second_sum, ("xh",), lambda a: (a + 1,))
    own_sum = own_terms(rows, weight)
    others = jnp.concatenate([got_first, got_second], axis=1)
    return (own_sum + others.astype(jnp.float32)).astype(jnp.bfloat16)


def solution(mesh):
    split = Mesh(mesh.devices.reshape([SIZES[a] for a in AXES]), AXES)
    seq, head = ("y", "xl", "c"), ("xh", "z")
    placed = (P(seq, head), P(seq, head), P(seq, head), P(seq), P(head, seq))
    return jax.shard_map(
        per_device, mesh=split, in_specs=placed, out_specs=P(seq, head), check_vma=False
    )
```

```python
import functools
import math

import jax
import jax.numpy as jnp
from jax import lax
from jax.experimental import pallas as pl
from jax.experimental.pallas import tpu as pltpu
from jax.sharding import Mesh
from jax.sharding import PartitionSpec as P

HD = 128
BLK = 128
TILE = 512
AXES = ("y", "xl", "c", "xh", "z")
SIZES = {"y": 4, "xl": 2, "c": 2, "xh": 2, "z": 4}
masked_score = -1e30
VMEM_BYTES = 56 << 20


def move(block, axes, target):
    sizes = [SIZES[a] for a in axes]
    count = math.prod(sizes)
    route = []
    for i in range(count):
        rest, at = i, []
        for size in reversed(sizes):
            at.append(rest % size)
            rest //= size
        to = target(*reversed(at))
        j = 0
        for t, size in zip(to, sizes):
            j = j * size + t % size
        route.append((i, j))
    return lax.ppermute(block, axes, route)


def run_all(copies):
    for copy in copies:
        copy.start()
    for copy in copies:
        copy.wait()


def sort_blocks(slot_ref, mine_ref, other_ref, sorted_ref, sem):
    run_all(
        [
            pltpu.make_async_copy(
                (mine_ref, other_ref)[i // 32].at[i // 4 % 8, pl.ds(i % 4 * 2 * BLK, 2 * BLK), :],
                sorted_ref.at[slot_ref[i]],
                sem.at[i],
            )
            for i in range(64)
        ]
    )


def sorted_kv(slots, mine, other):
    anywhere = pl.BlockSpec(memory_space=pl.ANY)
    return pl.pallas_call(
        sort_blocks,
        out_shape=jax.ShapeDtypeStruct((64, 2 * BLK, HD), jnp.bfloat16),
        in_specs=[pl.BlockSpec(memory_space=pltpu.SMEM), anywhere, anywhere],
        out_specs=pl.BlockSpec(memory_space=pltpu.VMEM),
        scratch_shapes=[pltpu.SemaphoreType.DMA((64,))],
        compiler_params=pltpu.CompilerParams(vmem_limit_bytes=VMEM_BYTES),
        cost_estimate=pl.CostEstimate(flops=0, bytes_accessed=8 << 20, transcendentals=0),
        name="sort_blocks",
    )(slots, mine, other)


def attend(chunk, heads, own_ref, order_ref, q_ref, kv_ref, out_ref, kv_s, q_s, s_s, acc, best, total, sem):
    rows = heads * BLK
    tile = TILE * 8 // heads
    per_tile = tile // BLK
    factor = math.log2(math.e) / math.sqrt(HD)
    block = own_ref[order_ref[chunk]]
    tiles = block // per_tile + 1

    def copy_of(j):
        slots = pl.ds(j * per_tile, per_tile)
        return pltpu.make_async_copy(kv_ref.at[slots], kv_s.at[slots], sem.at[j])

    def begin(j, carry):
        copy_of(j).start()
        return carry

    lax.fori_loop(0, tiles, begin, 0)
    for h in range(heads):
        q_s[h * BLK : (h + 1) * BLK, :] = q_ref[:, h * HD : (h + 1) * HD]
    acc[...] = jnp.zeros_like(acc)
    best[...] = jnp.full_like(best, masked_score)
    total[...] = jnp.zeros_like(total)

    def score(j):
        return lax.dot_general(
            kv_s[pl.ds(j * per_tile, per_tile), :BLK, :].reshape(tile, HD),
            q_s[...],
            (((1,), (1,)), ((), ())),
            preferred_element_type=jnp.float32,
        )

    def absorb(j, scores):
        old = best[...]
        new = jnp.maximum(old, jnp.max(scores, axis=0, keepdims=True))
        weights = jnp.exp2((scores - new) * factor)
        shrink = jnp.exp2((old - new) * factor)
        total[...] = total[...] * shrink + jnp.sum(weights, axis=0, keepdims=True)
        best[...] = new
        acc[...] = acc[...] * shrink + lax.dot_general(
            kv_s[pl.ds(j * per_tile, per_tile), BLK:, :].reshape(tile, HD),
            weights.astype(jnp.bfloat16),
            (((0,), (0,)), ((), ())),
            preferred_element_type=jnp.float32,
        )

    copy_of(0).wait()
    s_s[0] = score(0)

    def full_tile(j, carry):
        copy_of(j + 1).wait()
        scores = s_s[j % 2]
        s_s[(j + 1) % 2] = score(j + 1)
        absorb(j, scores)
        return carry

    lax.fori_loop(0, tiles - 1, full_tile, 0)
    last = tiles - 1
    key_at = last * tile + lax.broadcasted_iota(jnp.int32, (tile, rows), 0)
    query_at = block * BLK + lax.broadcasted_iota(jnp.int32, (tile, rows), 1) % BLK
    absorb(last, jnp.where(key_at <= query_at, s_s[last % 2], masked_score))
    result = acc[...] / total[...]
    for h in range(heads):
        part = result[:, h * BLK : (h + 1) * BLK]
        out_ref[:, h * HD : (h + 1) * HD] = part.T.astype(jnp.bfloat16)


def attention(chunk, part, heads, own, order, queries, kv):
    rows = heads * BLK
    tile = TILE * 8 // heads
    return pl.pallas_call(
        functools.partial(attend, chunk, heads),
        out_shape=jax.ShapeDtypeStruct((BLK, heads * HD), jnp.bfloat16),
        grid_spec=pltpu.PrefetchScalarGridSpec(
            num_scalar_prefetch=2,
            grid=(1,),
            in_specs=[
                pl.BlockSpec((BLK, heads * HD), lambda i, own, order: (order[chunk], part)),
                pl.BlockSpec(memory_space=pl.ANY),
            ],
            out_specs=pl.BlockSpec((BLK, heads * HD), lambda i, own, order: (0, 0)),
            scratch_shapes=[
                pltpu.VMEM((64, 2 * BLK, HD), jnp.bfloat16),
                pltpu.VMEM((rows, HD), jnp.bfloat16),
                pltpu.VMEM((2, tile, rows), jnp.float32),
                pltpu.VMEM((HD, rows), jnp.float32),
                pltpu.VMEM((1, rows), jnp.float32),
                pltpu.VMEM((1, rows), jnp.float32),
                pltpu.SemaphoreType.DMA((64 * BLK // tile,)),
            ],
        ),
        compiler_params=pltpu.CompilerParams(vmem_limit_bytes=VMEM_BYTES),
        cost_estimate=pl.CostEstimate(
            flops=1_250_000_000 * heads, bytes_accessed=1 << 22, transcendentals=0
        ),
        name="attend",
    )(own, order, queries, kv)


def collect_rows(places, order_ref, *refs):
    pieces, (rows_ref, sem) = refs[:-2], refs[-2:]
    run_all(
        [
            pltpu.make_async_copy(
                piece,
                rows_ref.at[
                    pl.ds(pl.multiple_of(order_ref[chunk] * BLK, BLK), BLK),
                    pl.ds(at, piece.shape[1]),
                ],
                sem.at[i],
            )
            for i, (piece, (chunk, at)) in enumerate(zip(pieces, places))
        ]
    )


def collected(order, pieces, places):
    return pl.pallas_call(
        functools.partial(collect_rows, places),
        out_shape=jax.ShapeDtypeStruct((512, 4096), jnp.bfloat16),
        in_specs=[pl.BlockSpec(memory_space=pltpu.SMEM)]
        + [pl.BlockSpec(memory_space=pl.ANY)] * len(pieces),
        out_specs=pl.BlockSpec(memory_space=pltpu.VMEM),
        scratch_shapes=[pltpu.SemaphoreType.DMA((len(pieces),))],
        compiler_params=pltpu.CompilerParams(vmem_limit_bytes=VMEM_BYTES),
        cost_estimate=pl.CostEstimate(flops=0, bytes_accessed=8 << 20, transcendentals=0),
        name="collect_rows",
    )(order, *pieces)


def project_partner(a_ref, w_ref, out_ref):
    w = w_ref[...].reshape(4096, 256)
    out = jnp.dot(a_ref[...], w, preferred_element_type=jnp.float32)
    out_ref[...] = out.astype(jnp.bfloat16)


def partner_terms(rows, weight):
    return pl.pallas_call(
        project_partner,
        out_shape=jax.ShapeDtypeStruct((512, 1024), jnp.bfloat16),
        grid=(4,),
        in_specs=[
            pl.BlockSpec((512, 4096), lambda n: (0, 0)),
            pl.BlockSpec((8, None, None, 512, 256), lambda n: (0, n // 2, 0, 0, n % 2)),
        ],
        out_specs=pl.BlockSpec((512, 256), lambda n: (0, n)),
        compiler_params=pltpu.CompilerParams(vmem_limit_bytes=VMEM_BYTES),
        cost_estimate=pl.CostEstimate(
            flops=2 * 512 * 4096 * 1024, bytes_accessed=13 << 20, transcendentals=0
        ),
        name="project_partner",
    )(rows, weight)


def project_self(a_ref, w_ref, out_ref):
    w = w_ref[...].reshape(4096, 256)
    out_ref[...] = jnp.dot(a_ref[...], w, preferred_element_type=jnp.float32)


def own_terms(rows, weight):
    return pl.pallas_call(
        project_self,
        out_shape=jax.ShapeDtypeStruct((512, 1024), jnp.float32),
        grid=(4,),
        in_specs=[
            pl.BlockSpec((512, 4096), lambda n: (0, 0)),
            pl.BlockSpec((8, None, None, 512, 256), lambda n: (0, n // 2, 1, 0, n % 2)),
        ],
        out_specs=pl.BlockSpec((512, 256), lambda n: (0, n)),
        compiler_params=pltpu.CompilerParams(vmem_limit_bytes=VMEM_BYTES),
        cost_estimate=pl.CostEstimate(
            flops=2 * 512 * 4096 * 1024, bytes_accessed=14 << 20, transcendentals=0
        ),
        name="project_self",
    )(rows, weight)


def spread_target(half):
    def target(y, xl, xh, z):
        plane = (y % 2) * 2 + xl
        other = (y // 2) ^ xh
        part = half if other else 1 - half
        return ((z - plane) % 4, part, xh, plane)

    return target


def swap_cores(block):
    return move(block, ("c",), lambda a: (a + 1,))


def per_device(queries, keys, values, positions, out_weight):
    y, xl, xh = lax.axis_index("y"), lax.axis_index("xl"), lax.axis_index("xh")
    own = positions[::BLK] // BLK
    index = jnp.arange(4, dtype=jnp.int32)
    rank = jnp.sum((own[None, :] < own[:, None]).astype(jnp.int32), axis=1)
    order = jnp.sum(jnp.where(rank[None, :] == index[:, None], index[None, :], 0), axis=1)
    ids = jnp.broadcast_to(own.astype(jnp.bfloat16)[None, :, None], (4, 4, HD)).reshape(16, HD)
    pairs = jnp.stack([keys.reshape(4, BLK, HD), values.reshape(4, BLK, HD)], 1)
    packet = jnp.concatenate([pairs.reshape(8 * BLK, HD), ids])
    copies = jnp.broadcast_to(packet[None], (8, *packet.shape))
    mine = lax.all_to_all(copies, ("y", "xl"), 0, 0, tiled=True)

    def later(first, *values):
        return lax.optimization_barrier((first, *values))[1:]

    other = (y // 2) ^ xh
    first = lax.dynamic_slice_in_dim(out_weight, (1 - other) * 512, 512, 0)
    second = lax.dynamic_slice_in_dim(out_weight, other * 512, 512, 0)
    plane = ("y", "xl", "xh", "z")
    got_first = move(first, plane, spread_target(0))
    got_second = move(second, plane, spread_target(1))
    got_first, got_second, mine = lax.optimization_barrier((got_first, got_second, mine))
    theirs = swap_cores(mine)
    both = jnp.where(xl == 0, jnp.stack([got_first, got_second]), jnp.stack([got_second, got_first]))
    weight = lax.all_gather(both.reshape(1024, 512), ("y", "xl", "c")).reshape(8, 2, 2, 512, 512)
    slots = jnp.concatenate([mine[:, 1024:1028, 0].reshape(32), theirs[:, 1024:1028, 0].reshape(32)])
    kv = sorted_kv(slots.astype(jnp.int32), mine, theirs)

    sets, places = [], []
    for chunk, part, heads in ((0, 0, 8), (1, 0, 8), (2, 0, 8), (3, 0, 4), (3, 1, 4)):
        if sets:
            (queries,) = later(sets[-1][0], queries)
        if len(sets) > 1:
            (queries,) = later(sets[-2][1:], queries)
        piece = attention(chunk, part, heads, own, order, queries, kv)
        around = [move(piece, ("z",), lambda a, dz=dz: (a - dz,)) for dz in (1, 2, 3)]
        sets.append([piece] + around)
        places += [(chunk, dz * 1024 + part * 512) for dz in range(4)]
    pieces = [piece for group in sets for piece in group]
    rows = collected(order, pieces, tuple(places))
    others = move(partner_terms(rows, weight), ("xh",), lambda a: (a + 1,))
    own_sum = own_terms(rows, weight)
    return (own_sum + others.astype(jnp.float32)).astype(jnp.bfloat16)


def solution(mesh):
    split = Mesh(mesh.devices.reshape([SIZES[a] for a in AXES]), AXES)
    seq, head = ("y", "xl", "c"), ("xh", "z")
    placed = (P(seq, head), P(seq, head), P(seq, head), P(seq), P(head, seq))
    return jax.shard_map(
        per_device, mesh=split, in_specs=placed, out_specs=P(seq, head), check_vma=False
    )
```

```python
import functools
import math

import jax
import jax.numpy as jnp
from jax import lax
from jax.experimental import pallas as pl
from jax.experimental.pallas import tpu as pltpu
from jax.sharding import Mesh
from jax.sharding import PartitionSpec as P

HD = 128
BLK = 128
TILE = 512
AXES = ("y", "xl", "c", "xh", "z")
SIZES = {"y": 4, "xl": 2, "c": 2, "xh": 2, "z": 4}
masked_score = -1e30
VMEM_BYTES = 56 << 20


def move(block, axes, target):
    sizes = [SIZES[a] for a in axes]
    count = math.prod(sizes)
    route = []
    for i in range(count):
        rest, at = i, []
        for size in reversed(sizes):
            at.append(rest % size)
            rest //= size
        to = target(*reversed(at))
        j = 0
        for t, size in zip(to, sizes):
            j = j * size + t % size
        route.append((i, j))
    return lax.ppermute(block, axes, route)


def run_all(copies):
    for copy in copies:
        copy.start()
    for copy in copies:
        copy.wait()


def sort_blocks(slot_ref, mine_ref, other_ref, sorted_ref, sem):
    run_all(
        [
            pltpu.make_async_copy(
                (mine_ref, other_ref)[i // 32].at[i // 4 % 8, pl.ds(i % 4 * 2 * BLK, 2 * BLK), :],
                sorted_ref.at[slot_ref[i]],
                sem.at[i],
            )
            for i in range(64)
        ]
    )


def sorted_kv(slots, mine, other):
    anywhere = pl.BlockSpec(memory_space=pl.ANY)
    return pl.pallas_call(
        sort_blocks,
        out_shape=jax.ShapeDtypeStruct((64, 2 * BLK, HD), jnp.bfloat16),
        in_specs=[pl.BlockSpec(memory_space=pltpu.SMEM), anywhere, anywhere],
        out_specs=pl.BlockSpec(memory_space=pltpu.VMEM),
        scratch_shapes=[pltpu.SemaphoreType.DMA((64,))],
        compiler_params=pltpu.CompilerParams(vmem_limit_bytes=VMEM_BYTES),
        cost_estimate=pl.CostEstimate(flops=0, bytes_accessed=8 << 20, transcendentals=0),
        name="sort_blocks",
    )(slots, mine, other)


def attend(chunk, heads, own_ref, order_ref, q_ref, kv_ref, out_ref, kv_s, q_s, s_s, acc, best, total, sem):
    rows = heads * BLK
    tile = TILE * 8 // heads
    per_tile = tile // BLK
    factor = math.log2(math.e) / math.sqrt(HD)
    block = own_ref[order_ref[chunk]]
    tiles = block // per_tile + 1

    def copy_of(j):
        slots = pl.ds(j * per_tile, per_tile)
        return pltpu.make_async_copy(kv_ref.at[slots], kv_s.at[slots], sem.at[j])

    def begin(j, carry):
        copy_of(j).start()
        return carry

    lax.fori_loop(0, tiles, begin, 0)
    for h in range(heads):
        q_s[h * BLK : (h + 1) * BLK, :] = q_ref[:, h * HD : (h + 1) * HD]
    acc[...] = jnp.zeros_like(acc)
    best[...] = jnp.full_like(best, masked_score)
    total[...] = jnp.zeros_like(total)

    def score(j):
        return lax.dot_general(
            kv_s[pl.ds(j * per_tile, per_tile), :BLK, :].reshape(tile, HD),
            q_s[...],
            (((1,), (1,)), ((), ())),
            preferred_element_type=jnp.float32,
        )

    def absorb(j, scores):
        old = best[...]
        new = jnp.maximum(old, jnp.max(scores, axis=0, keepdims=True))
        weights = jnp.exp2((scores - new) * factor)
        shrink = jnp.exp2((old - new) * factor)
        total[...] = total[...] * shrink + jnp.sum(weights, axis=0, keepdims=True)
        best[...] = new
        acc[...] = acc[...] * shrink + lax.dot_general(
            kv_s[pl.ds(j * per_tile, per_tile), BLK:, :].reshape(tile, HD),
            weights.astype(jnp.bfloat16),
            (((0,), (0,)), ((), ())),
            preferred_element_type=jnp.float32,
        )

    copy_of(0).wait()
    s_s[0] = score(0)

    def full_tile(j, carry):
        copy_of(j + 1).wait()
        scores = s_s[j % 2]
        s_s[(j + 1) % 2] = score(j + 1)
        absorb(j, scores)
        return carry

    lax.fori_loop(0, tiles - 1, full_tile, 0)
    last = tiles - 1
    key_at = last * tile + lax.broadcasted_iota(jnp.int32, (tile, rows), 0)
    query_at = block * BLK + lax.broadcasted_iota(jnp.int32, (tile, rows), 1) % BLK
    absorb(last, jnp.where(key_at <= query_at, s_s[last % 2], masked_score))
    result = acc[...] / total[...]
    for h in range(heads):
        part = result[:, h * BLK : (h + 1) * BLK]
        out_ref[:, h * HD : (h + 1) * HD] = part.T.astype(jnp.bfloat16)


def attention(chunk, part, heads, own, order, queries, kv):
    rows = heads * BLK
    tile = TILE * 8 // heads
    return pl.pallas_call(
        functools.partial(attend, chunk, heads),
        out_shape=jax.ShapeDtypeStruct((BLK, heads * HD), jnp.bfloat16),
        grid_spec=pltpu.PrefetchScalarGridSpec(
            num_scalar_prefetch=2,
            grid=(1,),
            in_specs=[
                pl.BlockSpec((BLK, heads * HD), lambda i, own, order: (order[chunk], part)),
                pl.BlockSpec(memory_space=pl.ANY),
            ],
            out_specs=pl.BlockSpec((BLK, heads * HD), lambda i, own, order: (0, 0)),
            scratch_shapes=[
                pltpu.VMEM((64, 2 * BLK, HD), jnp.bfloat16),
                pltpu.VMEM((rows, HD), jnp.bfloat16),
                pltpu.VMEM((2, tile, rows), jnp.float32),
                pltpu.VMEM((HD, rows), jnp.float32),
                pltpu.VMEM((1, rows), jnp.float32),
                pltpu.VMEM((1, rows), jnp.float32),
                pltpu.SemaphoreType.DMA((64 * BLK // tile,)),
            ],
        ),
        compiler_params=pltpu.CompilerParams(vmem_limit_bytes=VMEM_BYTES),
        cost_estimate=pl.CostEstimate(
            flops=1_250_000_000 * heads, bytes_accessed=1 << 22, transcendentals=0
        ),
        name="attend",
    )(own, order, queries, kv)


def collect_rows(places, order_ref, *refs):
    pieces, (rows_ref, sem) = refs[:-2], refs[-2:]
    run_all(
        [
            pltpu.make_async_copy(
                piece,
                rows_ref.at[
                    pl.ds(pl.multiple_of(order_ref[chunk] * BLK, BLK), BLK),
                    pl.ds(at, piece.shape[1]),
                ],
                sem.at[i],
            )
            for i, (piece, (chunk, at)) in enumerate(zip(pieces, places))
        ]
    )


def collected(order, pieces, places):
    return pl.pallas_call(
        functools.partial(collect_rows, places),
        out_shape=jax.ShapeDtypeStruct((512, 4096), jnp.bfloat16),
        in_specs=[pl.BlockSpec(memory_space=pltpu.SMEM)]
        + [pl.BlockSpec(memory_space=pl.ANY)] * len(pieces),
        out_specs=pl.BlockSpec(memory_space=pltpu.VMEM),
        scratch_shapes=[pltpu.SemaphoreType.DMA((len(pieces),))],
        compiler_params=pltpu.CompilerParams(vmem_limit_bytes=VMEM_BYTES),
        cost_estimate=pl.CostEstimate(flops=0, bytes_accessed=8 << 20, transcendentals=0),
        name="collect_rows",
    )(order, *pieces)


def project_partner(places, order_ref, *refs):
    pieces, (most_ref, w_ref, out_ref, all_ref, a_s, sem) = refs[:-6], refs[-6:]
    n = pl.program_id(0)
    keep = pltpu.make_async_copy(a_s, all_ref, sem.at[len(pieces)])

    @pl.when(n == 0)
    def _():
        run_all([pltpu.make_async_copy(most_ref, a_s, sem.at[len(pieces) + 1])])
        run_all(
            [
                pltpu.make_async_copy(
                    piece,
                    a_s.at[
                        pl.ds(pl.multiple_of(order_ref[chunk] * BLK, BLK), BLK),
                        pl.ds(at, piece.shape[1]),
                    ],
                    sem.at[i],
                )
                for i, (piece, (chunk, at)) in enumerate(zip(pieces, places))
            ]
        )
        keep.start()

    w = w_ref[...].reshape(4096, 256)
    out = jnp.dot(a_s[...], w, preferred_element_type=jnp.float32)
    out_ref[...] = out.astype(jnp.bfloat16)

    @pl.when(n == pl.num_programs(0) - 1)
    def _():
        keep.wait()


def partner_terms(order, most, pieces, places, weight):
    return pl.pallas_call(
        functools.partial(project_partner, places),
        out_shape=(
            jax.ShapeDtypeStruct((512, 512), jnp.bfloat16),
            jax.ShapeDtypeStruct((512, 4096), jnp.bfloat16),
        ),
        grid_spec=pltpu.PrefetchScalarGridSpec(
            num_scalar_prefetch=1,
            grid=(2,),
            in_specs=[pl.BlockSpec(memory_space=pl.ANY)] * (len(pieces) + 1)
            + [pl.BlockSpec((8, None, None, 512, 256), lambda n, o: (0, 0, 0, 0, n))],
            out_specs=(
                pl.BlockSpec((512, 256), lambda n, o: (0, n)),
                pl.BlockSpec(memory_space=pl.ANY),
            ),
            scratch_shapes=[
                pltpu.VMEM((512, 4096), jnp.bfloat16),
                pltpu.SemaphoreType.DMA((len(pieces) + 2,)),
            ],
        ),
        compiler_params=pltpu.CompilerParams(vmem_limit_bytes=VMEM_BYTES),
        cost_estimate=pl.CostEstimate(
            flops=2 * 512 * 4096 * 512, bytes_accessed=14 << 20, transcendentals=0
        ),
        name="project_partner",
    )(order, *pieces, most, weight)


def project_rest(a_ref, w_ref, out_ref):
    w = w_ref[...].reshape(4096, 256)
    out = jnp.dot(a_ref[...], w, preferred_element_type=jnp.float32)
    out_ref[...] = out.astype(jnp.bfloat16)


def rest_terms(rows, weight):
    return pl.pallas_call(
        project_rest,
        out_shape=jax.ShapeDtypeStruct((512, 512), jnp.bfloat16),
        grid=(2,),
        in_specs=[
            pl.BlockSpec((512, 4096), lambda n: (0, 0)),
            pl.BlockSpec((8, None, None, 512, 256), lambda n: (0, 1, 0, 0, n)),
        ],
        out_specs=pl.BlockSpec((512, 256), lambda n: (0, n)),
        compiler_params=pltpu.CompilerParams(vmem_limit_bytes=VMEM_BYTES),
        cost_estimate=pl.CostEstimate(
            flops=2 * 512 * 4096 * 512, bytes_accessed=9 << 20, transcendentals=0
        ),
        name="project_rest",
    )(rows, weight)


def project_self(a_ref, w_ref, out_ref):
    w = w_ref[...].reshape(4096, 256)
    out_ref[...] = jnp.dot(a_ref[...], w, preferred_element_type=jnp.float32)


def own_terms(rows, weight):
    return pl.pallas_call(
        project_self,
        out_shape=jax.ShapeDtypeStruct((512, 1024), jnp.float32),
        grid=(4,),
        in_specs=[
            pl.BlockSpec((512, 4096), lambda n: (0, 0)),
            pl.BlockSpec((8, None, None, 512, 256), lambda n: (0, n // 2, 1, 0, n % 2)),
        ],
        out_specs=pl.BlockSpec((512, 256), lambda n: (0, n)),
        compiler_params=pltpu.CompilerParams(vmem_limit_bytes=VMEM_BYTES),
        cost_estimate=pl.CostEstimate(
            flops=2 * 512 * 4096 * 1024, bytes_accessed=14 << 20, transcendentals=0
        ),
        name="project_self",
    )(rows, weight)


def spread_target(half):
    def target(y, xl, xh, z):
        plane = (y % 2) * 2 + xl
        other = (y // 2) ^ xh
        part = half if other else 1 - half
        return ((z - plane) % 4, part, xh, plane)

    return target


def swap_cores(block):
    return move(block, ("c",), lambda a: (a + 1,))


def per_device(queries, keys, values, positions, out_weight):
    y, xl, xh = lax.axis_index("y"), lax.axis_index("xl"), lax.axis_index("xh")
    own = positions[::BLK] // BLK
    index = jnp.arange(4, dtype=jnp.int32)
    rank = jnp.sum((own[None, :] < own[:, None]).astype(jnp.int32), axis=1)
    order = jnp.sum(jnp.where(rank[None, :] == index[:, None], index[None, :], 0), axis=1)
    ids = jnp.broadcast_to(own.astype(jnp.bfloat16)[None, :, None], (4, 4, HD)).reshape(16, HD)
    pairs = jnp.stack([keys.reshape(4, BLK, HD), values.reshape(4, BLK, HD)], 1)
    packet = jnp.concatenate([pairs.reshape(8 * BLK, HD), ids])
    copies = jnp.broadcast_to(packet[None], (8, *packet.shape))
    mine = lax.all_to_all(copies, ("y", "xl"), 0, 0, tiled=True)

    def later(first, *values):
        return lax.optimization_barrier((first, *values))[1:]

    other = (y // 2) ^ xh
    first = lax.dynamic_slice_in_dim(out_weight, (1 - other) * 512, 512, 0)
    second = lax.dynamic_slice_in_dim(out_weight, other * 512, 512, 0)
    plane = ("y", "xl", "xh", "z")
    got_first = move(first, plane, spread_target(0))
    got_second = move(second, plane, spread_target(1))
    got_first, got_second, mine = lax.optimization_barrier((got_first, got_second, mine))
    theirs = swap_cores(mine)
    both = jnp.where(xl == 0, jnp.stack([got_first, got_second]), jnp.stack([got_second, got_first]))
    weight = lax.all_gather(both.reshape(1024, 512), ("y", "xl", "c")).reshape(8, 2, 2, 512, 512)
    slots = jnp.concatenate([mine[:, 1024:1028, 0].reshape(32), theirs[:, 1024:1028, 0].reshape(32)])
    kv = sorted_kv(slots.astype(jnp.int32), mine, theirs)

    sets, places = [], []
    for chunk, part, heads in ((0, 0, 8), (1, 0, 8), (2, 0, 8), (3, 0, 4), (3, 1, 4)):
        if sets:
            (queries,) = later(sets[-1][0], queries)
        if len(sets) > 1:
            (queries,) = later(sets[-2][1:], queries)
        piece = attention(chunk, part, heads, own, order, queries, kv)
        around = [move(piece, ("z",), lambda a, dz=dz: (a - dz,)) for dz in (1, 2, 3)]
        sets.append([piece] + around)
        places += [(chunk, dz * 1024 + part * 512) for dz in range(4)]
    pieces = [piece for group in sets for piece in group]
    most = collected(order, pieces[:16], tuple(places[:16]))
    first_sum, rows = partner_terms(order, most, pieces[16:], tuple(places[16:]), weight)
    got_first = move(first_sum, ("xh",), lambda a: (a + 1,))
    got_second = move(rest_terms(rows, weight), ("xh",), lambda a: (a + 1,))
    (rows,) = later(got_first, rows)
    own_sum = own_terms(rows, weight)
    others = jnp.concatenate([got_first, got_second], axis=1)
    return (own_sum + others.astype(jnp.float32)).astype(jnp.bfloat16)


def solution(mesh):
    split = Mesh(mesh.devices.reshape([SIZES[a] for a in AXES]), AXES)
    seq, head = ("y", "xl", "c"), ("xh", "z")
    placed = (P(seq, head), P(seq, head), P(seq, head), P(seq), P(head, seq))
    return jax.shard_map(
        per_device, mesh=split, in_specs=placed, out_specs=P(seq, head), check_vma=False
    )
```

```python
import functools
import math

import jax
import jax.numpy as jnp
from jax import lax
from jax.experimental import pallas as pl
from jax.experimental.pallas import tpu as pltpu
from jax.sharding import Mesh
from jax.sharding import PartitionSpec as P

HD = 128
BLK = 128
TILE = 512
AXES = ("y", "xl", "c", "xh", "z")
SIZES = {"y": 4, "xl": 2, "c": 2, "xh": 2, "z": 4}
masked_score = -1e30
VMEM_BYTES = 56 << 20


def move(block, axes, target):
    sizes = [SIZES[a] for a in axes]
    count = math.prod(sizes)
    route = []
    for i in range(count):
        rest, at = i, []
        for size in reversed(sizes):
            at.append(rest % size)
            rest //= size
        to = target(*reversed(at))
        j = 0
        for t, size in zip(to, sizes):
            j = j * size + t % size
        route.append((i, j))
    return lax.ppermute(block, axes, route)


def run_all(copies):
    for copy in copies:
        copy.start()
    for copy in copies:
        copy.wait()


def sort_blocks(slot_ref, mine_ref, other_ref, sorted_ref, sem):
    run_all(
        [
            pltpu.make_async_copy(
                (mine_ref, other_ref)[i // 32].at[i // 4 % 8, pl.ds(i % 4 * 2 * BLK, 2 * BLK), :],
                sorted_ref.at[slot_ref[i]],
                sem.at[i],
            )
            for i in range(64)
        ]
    )


def sorted_kv(slots, mine, other):
    anywhere = pl.BlockSpec(memory_space=pl.ANY)
    return pl.pallas_call(
        sort_blocks,
        out_shape=jax.ShapeDtypeStruct((64, 2 * BLK, HD), jnp.bfloat16),
        in_specs=[pl.BlockSpec(memory_space=pltpu.SMEM), anywhere, anywhere],
        out_specs=pl.BlockSpec(memory_space=pltpu.VMEM),
        scratch_shapes=[pltpu.SemaphoreType.DMA((64,))],
        compiler_params=pltpu.CompilerParams(vmem_limit_bytes=VMEM_BYTES),
        cost_estimate=pl.CostEstimate(flops=0, bytes_accessed=8 << 20, transcendentals=0),
        name="sort_blocks",
    )(slots, mine, other)


def attend(chunk, heads, own_ref, order_ref, q_ref, kv_ref, out_ref, kv_s, q_s, s_s, acc, best, total, sem):
    rows = heads * BLK
    tile = TILE * 8 // heads
    per_tile = tile // BLK
    factor = math.log2(math.e) / math.sqrt(HD)
    block = own_ref[order_ref[chunk]]
    tiles = block // per_tile + 1

    def copy_of(j):
        slots = pl.ds(j * per_tile, per_tile)
        return pltpu.make_async_copy(kv_ref.at[slots], kv_s.at[slots], sem.at[j])

    def begin(j, carry):
        copy_of(j).start()
        return carry

    lax.fori_loop(0, tiles, begin, 0)
    for h in range(heads):
        q_s[h * BLK : (h + 1) * BLK, :] = q_ref[:, h * HD : (h + 1) * HD]
    acc[...] = jnp.zeros_like(acc)
    best[...] = jnp.full_like(best, masked_score)
    total[...] = jnp.zeros_like(total)

    def score(j):
        return lax.dot_general(
            kv_s[pl.ds(j * per_tile, per_tile), :BLK, :].reshape(tile, HD),
            q_s[...],
            (((1,), (1,)), ((), ())),
            preferred_element_type=jnp.float32,
        )

    def absorb(j, scores):
        old = best[...]
        new = jnp.maximum(old, jnp.max(scores, axis=0, keepdims=True))
        weights = jnp.exp2((scores - new) * factor)
        shrink = jnp.exp2((old - new) * factor)
        total[...] = total[...] * shrink + jnp.sum(weights, axis=0, keepdims=True)
        best[...] = new
        acc[...] = acc[...] * shrink + lax.dot_general(
            kv_s[pl.ds(j * per_tile, per_tile), BLK:, :].reshape(tile, HD),
            weights.astype(jnp.bfloat16),
            (((0,), (0,)), ((), ())),
            preferred_element_type=jnp.float32,
        )

    copy_of(0).wait()
    s_s[0] = score(0)

    def full_tile(j, carry):
        copy_of(j + 1).wait()
        scores = s_s[j % 2]
        s_s[(j + 1) % 2] = score(j + 1)
        absorb(j, scores)
        return carry

    lax.fori_loop(0, tiles - 1, full_tile, 0)
    last = tiles - 1
    key_at = last * tile + lax.broadcasted_iota(jnp.int32, (tile, rows), 0)
    query_at = block * BLK + lax.broadcasted_iota(jnp.int32, (tile, rows), 1) % BLK
    absorb(last, jnp.where(key_at <= query_at, s_s[last % 2], masked_score))
    result = acc[...] / total[...]
    for h in range(heads):
        part = result[:, h * BLK : (h + 1) * BLK]
        out_ref[:, h * HD : (h + 1) * HD] = part.T.astype(jnp.bfloat16)


def attention(chunk, part, heads, own, order, queries, kv):
    rows = heads * BLK
    tile = TILE * 8 // heads
    return pl.pallas_call(
        functools.partial(attend, chunk, heads),
        out_shape=jax.ShapeDtypeStruct((BLK, heads * HD), jnp.bfloat16),
        grid_spec=pltpu.PrefetchScalarGridSpec(
            num_scalar_prefetch=2,
            grid=(1,),
            in_specs=[
                pl.BlockSpec((BLK, heads * HD), lambda i, own, order: (order[chunk], part)),
                pl.BlockSpec(memory_space=pl.ANY),
            ],
            out_specs=pl.BlockSpec((BLK, heads * HD), lambda i, own, order: (0, 0)),
            scratch_shapes=[
                pltpu.VMEM((64, 2 * BLK, HD), jnp.bfloat16),
                pltpu.VMEM((rows, HD), jnp.bfloat16),
                pltpu.VMEM((2, tile, rows), jnp.float32),
                pltpu.VMEM((HD, rows), jnp.float32),
                pltpu.VMEM((1, rows), jnp.float32),
                pltpu.VMEM((1, rows), jnp.float32),
                pltpu.SemaphoreType.DMA((64 * BLK // tile,)),
            ],
        ),
        compiler_params=pltpu.CompilerParams(vmem_limit_bytes=VMEM_BYTES),
        cost_estimate=pl.CostEstimate(
            flops=1_250_000_000 * heads, bytes_accessed=1 << 22, transcendentals=0
        ),
        name="attend",
    )(own, order, queries, kv)


def collect_rows(places, order_ref, *refs):
    pieces, (rows_ref, sem) = refs[:-2], refs[-2:]
    run_all(
        [
            pltpu.make_async_copy(
                piece,
                rows_ref.at[
                    pl.ds(pl.multiple_of(order_ref[chunk] * BLK, BLK), BLK),
                    pl.ds(at, piece.shape[1]),
                ],
                sem.at[i],
            )
            for i, (piece, (chunk, at)) in enumerate(zip(pieces, places))
        ]
    )


def collected(order, pieces, places):
    return pl.pallas_call(
        functools.partial(collect_rows, places),
        out_shape=jax.ShapeDtypeStruct((512, 4096), jnp.bfloat16),
        in_specs=[pl.BlockSpec(memory_space=pltpu.SMEM)]
        + [pl.BlockSpec(memory_space=pl.ANY)] * len(pieces),
        out_specs=pl.BlockSpec(memory_space=pltpu.VMEM),
        scratch_shapes=[pltpu.SemaphoreType.DMA((len(pieces),))],
        compiler_params=pltpu.CompilerParams(vmem_limit_bytes=VMEM_BYTES),
        cost_estimate=pl.CostEstimate(flops=0, bytes_accessed=8 << 20, transcendentals=0),
        name="collect_rows",
    )(order, *pieces)


def project_partner(places, order_ref, *refs):
    pieces, (most_ref, w_ref, out_ref, all_ref, a_s, sem) = refs[:-6], refs[-6:]
    n = pl.program_id(0)
    keep = pltpu.make_async_copy(a_s, all_ref, sem.at[len(pieces)])

    @pl.when(n == 0)
    def _():
        run_all([pltpu.make_async_copy(most_ref, a_s, sem.at[len(pieces) + 1])])
        run_all(
            [
                pltpu.make_async_copy(
                    piece,
                    a_s.at[
                        pl.ds(pl.multiple_of(order_ref[chunk] * BLK, BLK), BLK),
                        pl.ds(at, piece.shape[1]),
                    ],
                    sem.at[i],
                )
                for i, (piece, (chunk, at)) in enumerate(zip(pieces, places))
            ]
        )
        keep.start()

    w = w_ref[...].reshape(4096, 256)
    out = jnp.dot(a_s[...], w, preferred_element_type=jnp.float32)
    out_ref[...] = out.astype(jnp.bfloat16)

    @pl.when(n == pl.num_programs(0) - 1)
    def _():
        keep.wait()


def partner_terms(order, most, pieces, places, weight):
    return pl.pallas_call(
        functools.partial(project_partner, places),
        out_shape=(
            jax.ShapeDtypeStruct((512, 512), jnp.bfloat16),
            jax.ShapeDtypeStruct((512, 4096), jnp.bfloat16),
        ),
        grid_spec=pltpu.PrefetchScalarGridSpec(
            num_scalar_prefetch=1,
            grid=(2,),
            in_specs=[pl.BlockSpec(memory_space=pl.ANY)] * (len(pieces) + 1)
            + [pl.BlockSpec((8, None, None, 512, 256), lambda n, o: (0, 0, 0, 0, n))],
            out_specs=(
                pl.BlockSpec((512, 256), lambda n, o: (0, n)),
                pl.BlockSpec(memory_space=pl.ANY),
            ),
            scratch_shapes=[
                pltpu.VMEM((512, 4096), jnp.bfloat16),
                pltpu.SemaphoreType.DMA((len(pieces) + 2,)),
            ],
        ),
        compiler_params=pltpu.CompilerParams(vmem_limit_bytes=VMEM_BYTES),
        cost_estimate=pl.CostEstimate(
            flops=2 * 512 * 4096 * 512, bytes_accessed=14 << 20, transcendentals=0
        ),
        name="project_partner",
    )(order, *pieces, most, weight)


def project_rest(a_ref, w_ref, out_ref):
    w = w_ref[...].reshape(4096, 256)
    out = jnp.dot(a_ref[...], w, preferred_element_type=jnp.float32)
    out_ref[...] = out.astype(jnp.bfloat16)


def rest_terms(rows, weight):
    return pl.pallas_call(
        project_rest,
        out_shape=jax.ShapeDtypeStruct((512, 512), jnp.bfloat16),
        grid=(2,),
        in_specs=[
            pl.BlockSpec((512, 4096), lambda n: (0, 0)),
            pl.BlockSpec((8, None, None, 512, 256), lambda n: (0, 1, 0, 0, n)),
        ],
        out_specs=pl.BlockSpec((512, 256), lambda n: (0, n)),
        compiler_params=pltpu.CompilerParams(vmem_limit_bytes=VMEM_BYTES),
        cost_estimate=pl.CostEstimate(
            flops=2 * 512 * 4096 * 512, bytes_accessed=9 << 20, transcendentals=0
        ),
        name="project_rest",
    )(rows, weight)


def project_self(a_ref, w_ref, out_ref):
    w = w_ref[...].reshape(4096, 256)
    out_ref[...] = jnp.dot(a_ref[...], w, preferred_element_type=jnp.float32)


def own_terms(rows, weight):
    return pl.pallas_call(
        project_self,
        out_shape=jax.ShapeDtypeStruct((512, 1024), jnp.float32),
        grid=(4,),
        in_specs=[
            pl.BlockSpec((512, 4096), lambda n: (0, 0)),
            pl.BlockSpec((8, None, None, 512, 256), lambda n: (0, n // 2, 1, 0, n % 2)),
        ],
        out_specs=pl.BlockSpec((512, 256), lambda n: (0, n)),
        compiler_params=pltpu.CompilerParams(vmem_limit_bytes=VMEM_BYTES),
        cost_estimate=pl.CostEstimate(
            flops=2 * 512 * 4096 * 1024, bytes_accessed=14 << 20, transcendentals=0
        ),
        name="project_self",
    )(rows, weight)


def spread_target(half):
    def target(y, xl, xh, z):
        plane = (y % 2) * 2 + xl
        other = (y // 2) ^ xh
        part = half if other else 1 - half
        return ((z - plane) % 4, part, xh, plane)

    return target


def swap_cores(block):
    return move(block, ("c",), lambda a: (a + 1,))


def per_device(queries, keys, values, positions, out_weight):
    y, xl, xh = lax.axis_index("y"), lax.axis_index("xl"), lax.axis_index("xh")
    own = positions[::BLK] // BLK
    index = jnp.arange(4, dtype=jnp.int32)
    rank = jnp.sum((own[None, :] < own[:, None]).astype(jnp.int32), axis=1)
    order = jnp.sum(jnp.where(rank[None, :] == index[:, None], index[None, :], 0), axis=1)
    ids = jnp.broadcast_to(own.astype(jnp.bfloat16)[None, :, None], (4, 4, HD)).reshape(16, HD)
    pairs = jnp.stack([keys.reshape(4, BLK, HD), values.reshape(4, BLK, HD)], 1)
    packet = jnp.concatenate([pairs.reshape(8 * BLK, HD), ids])
    copies = jnp.broadcast_to(packet[None], (8, *packet.shape))
    mine = lax.all_to_all(copies, ("y", "xl"), 0, 0, tiled=True)

    def later(first, *values):
        return lax.optimization_barrier((first, *values))[1:]

    other = (y // 2) ^ xh
    first = lax.dynamic_slice_in_dim(out_weight, (1 - other) * 512, 512, 0)
    plane = ("y", "xl", "xh", "z")
    got_first = move(first, plane, spread_target(0))
    got_first, mine = lax.optimization_barrier((got_first, mine))
    (rest_weight,) = later(mine, out_weight)
    second = lax.dynamic_slice_in_dim(rest_weight, other * 512, 512, 0)
    got_second = move(second, plane, spread_target(1))
    theirs = swap_cores(mine)
    slots = jnp.concatenate([mine[:, 1024:1028, 0].reshape(32), theirs[:, 1024:1028, 0].reshape(32)])
    kv = sorted_kv(slots.astype(jnp.int32), mine, theirs)
    got_first, got_second = later(kv, got_first, got_second)
    both = jnp.where(xl == 0, jnp.stack([got_first, got_second]), jnp.stack([got_second, got_first]))
    weight = lax.all_gather(both.reshape(1024, 512), ("y", "xl", "c")).reshape(8, 2, 2, 512, 512)

    sets, places = [], []
    for chunk, part, heads in ((0, 0, 8), (1, 0, 8), (2, 0, 8), (3, 0, 4), (3, 1, 4)):
        if sets:
            (queries,) = later(sets[-1][0], queries)
        if len(sets) > 1:
            (queries,) = later(sets[-2][1:], queries)
        piece = attention(chunk, part, heads, own, order, queries, kv)
        around = [move(piece, ("z",), lambda a, dz=dz: (a - dz,)) for dz in (1, 2, 3)]
        sets.append([piece] + around)
        places += [(chunk, dz * 1024 + part * 512) for dz in range(4)]
    pieces = [piece for group in sets for piece in group]
    most = collected(order, pieces[:16], tuple(places[:16]))
    first_sum, rows = partner_terms(order, most, pieces[16:], tuple(places[16:]), weight)
    got_first = move(first_sum, ("xh",), lambda a: (a + 1,))
    got_second = move(rest_terms(rows, weight), ("xh",), lambda a: (a + 1,))
    (rows,) = later(got_first, rows)
    own_sum = own_terms(rows, weight)
    others = jnp.concatenate([got_first, got_second], axis=1)
    return (own_sum + others.astype(jnp.float32)).astype(jnp.bfloat16)


def solution(mesh):
    split = Mesh(mesh.devices.reshape([SIZES[a] for a in AXES]), AXES)
    seq, head = ("y", "xl", "c"), ("xh", "z")
    placed = (P(seq, head), P(seq, head), P(seq, head), P(seq), P(head, seq))
    return jax.shard_map(
        per_device, mesh=split, in_specs=placed, out_specs=P(seq, head), check_vma=False
    )
```
